128 devices in a mesh: gx: 4 (over z), gy: 32 (over y, x, core).
Axes of the slice: x: 4, y: 4, z: 4, core: 2. Of those that a mesh axis runs over, the one named last changes fastest.
Arguments:
- positions: float32 [3, 262144], P(None, ('gx', 'gy')), may hold values from -1 to 1
- normals: float32 [3, 262144], P(None, ('gx', 'gy')), may hold values from -4 to 4
- emission: float32 [16, 262144], P(None, ('gx', 'gy')), may hold values from 0.05 to 2
- material: int32 [262144], P(('gx', 'gy')), may hold values from 0 to 7
- area_level: int32 [262144], P(('gx', 'gy')), may hold values from 0 to 7
- reflect_table: float32 [8, 16], replicated, may hold values from 0.1 to 0.9
- area_table: float32 [8], replicated, may hold values from 0.002 to 0.008
- pair_slots: int32 [128, 128, 2, 2], P(('gx', 'gy')), may hold values from -1 to 7, as said below
Outputs:
- radiosity: float32 [16, 262144], P(None, ('gx', 'gy'))
The draws below stay inside these ranges and needn't reach their ends.
Inputs may be any that keep to these rules, and one draw needn't show every extreme that they name: `pair_slots`: in slot [q, p, c], a row entry is -1 exactly when its column entry is -1; the non-empty slots of one [q, p] come first, at most 2 of them, and the slot group [q, q] is always full. No unordered pair of blocks occurs twice, and a slot never names the same block twice.
All inputs are finite; a program needn't handle non-finite values.
Results may differ from the reference program's by a relative error of at most 0.0017.
Values may be sent and summed in bfloat16 or wider, within the bound.
A program may use at most 64 MiB of HBM per device.

```python
import math
import jax
import jax.numpy as jnp
from jax import lax

BANDS = 16
BLK = 256
BLOCKS_DEV = 8
CAP = 2
ITERS = 2
MATS = 8
LEVELS = 8
PATCHES = 262144
N_GX = 4
N_GY = 32


def draw_pair_slots(key, part):
    total_dev = N_GX * N_GY
    half = BLOCKS_DEV // 2
    key_count = jax.random.fold_in(key, 11)
    key_offset = jax.random.fold_in(key, 12)
    key_column = jax.random.fold_in(key, 13)
    owner = jnp.arange(total_dev, dtype=jnp.int32)[:, None]
    peer = jnp.arange(total_dev, dtype=jnp.int32)[None, :]
    counts = jax.random.randint(key_count, (total_dev, total_dev), 0, CAP + 1, dtype=jnp.int32)
    counts = jnp.where(owner == peer, CAP, counts)
    offset = jax.random.randint(key_offset, (total_dev, total_dev), 0, half, dtype=jnp.int32)
    slot_ids = jnp.arange(CAP, dtype=jnp.int32)
    row_low = (offset[:, :, None] + slot_ids[None, None, :]) % half
    col_low = jax.random.randint(key_column, (total_dev, total_dev, CAP), 0, half, dtype=jnp.int32)
    below = (owner < peer)[:, :, None]
    above = (owner > peer)[:, :, None]
    row_pick = jnp.where(above, row_low + half, row_low)
    col_pick = jnp.where(below, col_low, col_low + half)
    filled = slot_ids[None, None, :] < counts[:, :, None]
    row_pick = jnp.where(filled, row_pick, -1)
    col_pick = jnp.where(filled, col_pick, -1)
    return jnp.stack([row_pick, col_pick], axis=-1).astype(jnp.int32)


def place_ends(array, stream_key, low, top_value):
    spot = [jax.random.randint(jax.random.fold_in(stream_key, axis), (), 0, length) for axis, length in enumerate(array.shape)]
    main_axis = array.shape.index(max(array.shape))
    next_to = spot[:main_axis] + [(spot[main_axis] + 1) % array.shape[main_axis]] + spot[main_axis + 1:]
    return array.at[tuple(spot)].set(low).at[tuple(next_to)].set(top_value)


def steps_of(own_key, shape, split, low, high):
    def one(dim, shards_of):
        heights = jax.random.uniform(jax.random.fold_in(jax.random.fold_in(own_key, 6), dim), (shards_of,), jnp.float32, low / len(split), high / len(split))
        return jnp.repeat(jnp.exp(heights), shape[dim] // shards_of).reshape((-1,) + (1,) * (len(shape) - dim - 1))

    gain = one(*split[0])
    for cut in split[1:]:
        gain = gain * one(*cut)
    return gain


def normal_values(key, dims, scale, limit, split=(), kind=jnp.bfloat16):
    factor_of = steps_of(key, dims, split, -0.22, 0.18) if split else 1.0
    result = jax.random.normal(key, dims, jnp.float32) * scale * factor_of
    return jnp.minimum(jnp.maximum(result, -limit), limit).astype(kind)


def setup_inputs(seed: int = 0) -> dict:
    splits = jax.random.split(jax.random.key(seed), 9)
    positions = jnp.clip(jax.random.uniform(splits[0], (3, PATCHES), jnp.float32, -1.0, 1.0) * steps_of(splits[0], (3, PATCHES), ((1, 128),), -0.4, 0.0), -1.0, 1.0)
    normals = normal_values(splits[1], (3, PATCHES), 1.0, 4.0, ((1, 128),), jnp.float32)
    emission = jnp.clip(jnp.exp(math.log(2.0) - 3.6888794 * jax.random.uniform(splits[2], (BANDS, PATCHES), jnp.float32) ** steps_of(splits[2], (BANDS, PATCHES), ((1, 128),), -0.2, 0.2)), 0.05, 2.0)
    material = place_ends(jax.random.randint(splits[3], (PATCHES,), 0, MATS), jax.random.fold_in(splits[3], 1), 0, MATS - 1).astype(jnp.int32)
    area_level = place_ends(jax.random.randint(splits[4], (PATCHES,), 0, LEVELS), jax.random.fold_in(splits[4], 1), 0, LEVELS - 1).astype(jnp.int32)
    reflect_table = jnp.clip(jax.random.uniform(splits[5], (MATS, BANDS), jnp.float32, 0.1, 0.9), 0.1, 0.9)
    area_table = jnp.clip(jnp.exp(jax.random.uniform(splits[6], (LEVELS,), jnp.float32, math.log(0.002), math.log(0.008))), 0.002, 0.008)
    pair_slots = draw_pair_slots(jax.random.fold_in(splits[8], 71), 0)
    return dict(positions=positions, normals=normals, emission=emission, material=material, area_level=area_level, reflect_table=reflect_table, area_table=area_table, pair_slots=pair_slots)


def view_tile(row_geo, col_geo):
    delta = [col_geo[k][None, :] - row_geo[k][:, None] for k in range(3)]
    squared = delta[0] * delta[0] + delta[1] * delta[1] + delta[2] * delta[2]
    facing = jnp.maximum(row_geo[3][:, None] * delta[0] + row_geo[4][:, None] * delta[1] + row_geo[5][:, None] * delta[2], 0.0)
    seen = jnp.maximum(-(col_geo[3][None, :] * delta[0] + col_geo[4][None, :] * delta[1] + col_geo[5][None, :] * delta[2]), 0.0)
    mean_area = 0.5 * (row_geo[6][:, None] + col_geo[6][None, :])
    return facing * seen / ((squared + mean_area) * (math.pi * squared + mean_area))


def reference(positions, normals, emission, material, area_level, reflect_table, area_table, pair_slots):
    total_dev = N_GX * N_GY
    nblocks = PATCHES // BLK
    area = area_table[area_level]
    reflect = jnp.transpose(reflect_table)[:, material]
    geometry = jnp.concatenate([positions, normals, area[None, :]], axis=0)
    geo_blocks = jnp.transpose(geometry.reshape(7, nblocks, BLK), (1, 0, 2))
    owner = jnp.broadcast_to(jnp.arange(total_dev, dtype=jnp.int32)[:, None, None], (total_dev, total_dev, CAP))
    peer = jnp.broadcast_to(jnp.arange(total_dev, dtype=jnp.int32)[None, :, None], (total_dev, total_dev, CAP))
    row_local = pair_slots[..., 0]
    col_local = pair_slots[..., 1]
    usable = (row_local >= 0).astype(jnp.float32)
    row_block = (owner * BLOCKS_DEV + jnp.maximum(row_local, 0)).astype(jnp.int32).reshape(-1, 32)
    col_block = (peer * BLOCKS_DEV + jnp.maximum(col_local, 0)).astype(jnp.int32).reshape(-1, 32)
    usable = usable.reshape(-1, 32)
    radiosity = emission
    for sweep in range(ITERS):
        flux = (area[None, :] * radiosity).astype(jnp.bfloat16)
        flux_blocks = jnp.transpose(flux.reshape(BANDS, nblocks, BLK), (1, 0, 2))

        def one_group(carry, item):
            rows_here, cols_here, mask_here = item
            tiles = jax.vmap(view_tile)(geo_blocks[rows_here], geo_blocks[cols_here])
            tiles = (tiles * mask_here[:, None, None]).astype(jnp.bfloat16).astype(jnp.float32)
            own = jnp.einsum('sbj,sij->sbi', flux_blocks[cols_here].astype(jnp.float32), tiles)
            back = jnp.einsum('sbi,sij->sbj', flux_blocks[rows_here].astype(jnp.float32), tiles)
            carry = carry.at[rows_here].add(own)
            carry = carry.at[cols_here].add(back)
            return carry, None

        start = jnp.zeros((nblocks, BANDS, BLK), jnp.float32)
        summed, unused = lax.scan(one_group, start, (row_block, col_block, usable))
        irradiation = jnp.transpose(summed, (1, 0, 2)).reshape(BANDS, PATCHES)
        radiosity = emission + reflect * irradiation
    return radiosity
```

```python
import functools
import math

import jax
import jax.numpy as jnp
from jax import lax
from jax.experimental import pallas as pl
from jax.experimental.pallas import tpu as pltpu
from jax.sharding import PartitionSpec as P

MESH = pl.DeviceIdType.MESH
BANDS = 16
BLK = 256
HALF = 128
ITERS = 2
AXES = ("gx", "gy")
SIDE = 4
ORDERS = (("x", "y", "z"), ("y", "z", "x"), ("z", "x", "y"))
FLUX_PARTS = (6, 5, 5)
GEO_PARTS = (5, 6, 5)
KEPT = 336
STEP = 4
STEP2 = 8
CHUNK = 64
KAPPA = (math.pi - 1.0) / math.pi


def my_place():
    z = lax.axis_index("gx")
    inner = lax.axis_index("gy")
    place = {"z": z, "y": lax.div(inner, 2 * SIDE), "x": lax.rem(lax.div(inner, 2), SIDE)}
    return place, lax.rem(inner, 2)


def device_of(place, core):
    return (place["z"], (place["y"] * SIDE + place["x"]) * 2 + core)


def moved(place, axis, by):
    other = dict(place)
    other[axis] = lax.rem(place[axis] + (by + SIDE), SIDE)
    return other


def gather_kernel(parts, count, *refs):
    srcs, bufs = refs[:count], refs[count : 2 * count]
    send_sem, recv_sem, local_sem = refs[2 * count :]
    here, core = my_place()
    other_core = device_of(here, 1 - core)
    own_copies = []
    for b in range(count):
        place = bufs[b].at[here["z"], here["y"], here["x"], core]
        own_copies.append(pltpu.make_async_copy(srcs[b], place, local_sem.at[b]))
        own_copies[-1].start()
    barrier = pltpu.get_barrier_semaphore()
    peers = [device_of(moved(here, axis, by), core) for axis in "zyx" for by in (1, -1)]
    peers.append(other_core)
    for peer in peers:
        pl.semaphore_signal(barrier, inc=1, device_id=peer, device_id_type=MESH)
    pl.semaphore_wait(barrier, len(peers))
    started = []
    shared = []

    def send(src, dst, to):
        n = len(started)
        copy = pltpu.make_async_remote_copy(
            src_ref=src,
            dst_ref=dst,
            send_sem=send_sem.at[n],
            recv_sem=recv_sem.at[n],
            device_id=to,
            device_id_type=MESH,
        )
        copy.start()
        started.append(copy)
        return copy

    def view(b, index, first, size):
        return bufs[b].at[index["z"], index["y"], index["x"], core, pl.ds(first, size)]

    def share(b, index, first, size):
        piece = view(b, index, first, size)
        shared.append(send(piece, piece, other_core))

    work = []
    for b in range(count):
        first = 0
        for k, size in enumerate(parts[b]):
            work.append((b, k, first, size))
            first += size

    def group(phase, k, by):
        order = ORDERS[k]
        index = moved(here, order[phase], by)
        for axis in order[:phase]:
            index[axis] = pl.ds(0, SIDE)
        return index

    def half_of(phase, k, index, first, size, which):
        if phase == 0:
            low = (size + 1) // 2
            return (index, first, low) if which == 0 else (index, first + low, size - low)
        index = dict(index)
        index[ORDERS[k][0]] = pl.ds(2 * which, 2)
        return index, first, size

    for phase in range(3):
        up, down, up2, down2 = {}, {}, {}, {}
        for item in work:
            b, k, first, size = item
            axis = ORDERS[k][phase]
            dst = view(b, group(phase, k, 0), first, size)
            src = dst if phase else srcs[b].at[pl.ds(first, size)]
            up[item] = send(src, dst, device_of(moved(here, axis, 1), core))
            down[item] = send(src, dst, device_of(moved(here, axis, -1), core))
        if phase == 0:
            for b in range(count):
                place = bufs[b].at[here["z"], here["y"], here["x"], core]
                shared.append(send(srcs[b], place, other_core))
            for copy in own_copies:
                copy.wait()
        for item in work:
            b, k, first, size = item
            axis = ORDERS[k][phase]
            below, above = group(phase, k, -1), group(phase, k, 1)
            up[item].wait_recv()
            piece = view(b, *half_of(phase, k, below, first, size, 0))
            up2[item] = send(piece, piece, device_of(moved(here, axis, 1), core))
            down[item].wait_recv()
            piece = view(b, *half_of(phase, k, above, first, size, 1))
            down2[item] = send(piece, piece, device_of(moved(here, axis, -1), core))
            share(b, below, first, size)
            share(b, above, first, size)
        for item in work:
            b, k, first, size = item
            up2[item].wait_recv()
            down2[item].wait_recv()
            share(b, group(phase, k, 2), first, size)
    for copy in shared:
        copy.wait_recv()
    for copy in started:
        copy.wait_send()


def gather_all(arrays, parts, collective_id):
    count = len(arrays)
    copies = (3 * 7 * 3 + 1) * count
    anywhere = pl.BlockSpec(memory_space=pl.ANY)
    return pl.pallas_call(
        functools.partial(gather_kernel, parts, count),
        out_shape=[
            jax.ShapeDtypeStruct((SIDE, SIDE, SIDE, 2) + a.shape, a.dtype) for a in arrays
        ],
        in_specs=[anywhere] * count,
        out_specs=[anywhere] * count,
        scratch_shapes=[
            pltpu.SemaphoreType.DMA((copies,)),
            pltpu.SemaphoreType.DMA((copies,)),
            pltpu.SemaphoreType.DMA((count,)),
        ],
        compiler_params=pltpu.CompilerParams(collective_id=collective_id, has_side_effects=True),
        name="gather_all",
    )(*arrays)


def split3(x):
    a = x.astype(jnp.bfloat16).astype(jnp.float32)
    rest = x - a
    b = rest.astype(jnp.bfloat16).astype(jnp.float32)
    return a, b, rest - b


def block_of(ref, b):
    return jnp.concatenate([ref[b, 0], ref[b, 1]], axis=1)


def centred(rows, centre):
    moved_rows = rows - centre
    squares = moved_rows * moved_rows
    cross = moved_rows * pltpu.roll(moved_rows, 4, 0)
    reach = (squares[0:1] + squares[1:2] + squares[2:3]) + 0.5 * rows[3:4]
    plane = -(cross[0:1] + cross[1:2] + cross[2:3])
    return moved_rows, reach, plane


def source_rows(rows, centre):
    at = lax.broadcasted_iota(jnp.int32, rows.shape, 0)
    base, reach, plane = centred(rows, centre)
    base = jnp.where(at == 3, reach, jnp.where(at == 7, plane, base))
    a, b, c = split3(base)
    one = jnp.where(at < 3, 1.0, 0.0)
    stacked = jnp.concatenate([a, a, a, b, b, c, one, jnp.zeros_like(one)], axis=0)
    return stacked.astype(jnp.bfloat16), (KAPPA * 0.5) * rows[3:4]


def target_columns(rows, centre):
    at = lax.broadcasted_iota(jnp.int32, rows.shape, 0)
    base, reach, plane = centred(rows, centre)
    zero = jnp.zeros_like(base)
    swapped = pltpu.roll(base, 4, 0)
    facing = jnp.where(at < 3, swapped, 0.0) * (1.0 / math.pi)
    seen = jnp.where((at >= 4) & (at < 7), swapped, jnp.where(at == 7, 1.0, 0.0))
    spread = jnp.where(at < 3, -2.0 * base, jnp.where(at == 3, 1.0, 0.0))
    columns = []
    for factor, constant in ((facing, plane * (1.0 / math.pi)), (seen, None), (spread, reach)):
        a, b, c = split3(factor)
        last = zero
        if constant is not None:
            d, e, f = split3(constant)
            last = jnp.where(at == 0, d, jnp.where(at == 1, e, jnp.where(at == 2, f, 0.0)))
        stacked = jnp.concatenate([a, b, c, a, b, a, last, zero], axis=0)
        columns.append(jnp.transpose(stacked).astype(jnp.bfloat16))
    return columns, (KAPPA * 0.5) * rows[3:4]


def prepare_targets(own_ref, centre_ref, column_ref, offset_ref):
    for t in range(8):
        rows = block_of(own_ref, t)
        at = lax.broadcasted_iota(jnp.int32, rows.shape, 0)
        centre = jnp.where(at < 3, jnp.broadcast_to(rows[:, 0:1], rows.shape), 0.0)
        centre_ref[t] = centre
        columns, offset = target_columns(rows, centre)
        for r in range(0, BLK, CHUNK):
            column_ref[t, 3 * r : 3 * (r + CHUNK)] = jnp.concatenate(
                [c[r : r + CHUNK] for c in columns], axis=0
            )
        offset_ref[t] = jnp.transpose(jnp.broadcast_to(offset, (HALF, BLK)))


def build_tile(t, b, geo_ref, centre_ref, column_ref, offset_ref, tile_ref, slot):
    source, source_offset = source_rows(block_of(geo_ref, b), centre_ref[t])
    for r in range(0, BLK, CHUNK):
        terms = jnp.dot(
            column_ref[t, 3 * r : 3 * (r + CHUNK), :], source, preferred_element_type=jnp.float32
        )
        facing, seen, spread = terms[:CHUNK], terms[CHUNK : 2 * CHUNK], terms[2 * CHUNK :]
        offset = offset_ref[t, r : r + CHUNK, :]
        offset = jnp.concatenate([offset, offset], axis=1)
        over = jnp.maximum(facing, 0.0) * jnp.maximum(seen, 0.0)
        under = spread * ((spread - offset) - source_offset)
        inverse = pl.reciprocal(under, approx=True)
        inverse = inverse * (2.0 - under * inverse)
        tile_ref[slot, r : r + CHUNK, :] = (over * inverse).astype(jnp.bfloat16)


def add_product(t, flux, tile, sum_ref):
    term = lax.dot_general(
        flux, tile, (((1,), (1,)), ((), ())), preferred_element_type=jnp.float32
    )
    sum_ref[t, 0] += term[:, :HALF]
    sum_ref[t, 1] += term[:, HALF:]


def decode(code):
    t = lax.shift_right_logical(code, 10)
    return t, jnp.minimum(t, 7), lax.bitwise_and(code, 1023)


def first_kernel(
    slot_ref, geo_ref, flux_ref, own_ref, emission_ref, reflect_ref, area_ref,
    leaving_ref, tiles_ref, list_ref, count_ref,
    centre_ref, column_ref, offset_ref, sum_ref, *rest,
):
    bufs, sem = rest[:STEP], rest[STEP]
    prepare_targets(own_ref, centre_ref, column_ref, offset_ref)
    sum_ref[...] = jnp.zeros_like(sum_ref)

    def compact(e, n):
        for k in range(8):
            code = slot_ref[e * 8 + k]
            list_ref[n] = code
            n = n + jnp.where(code >= 0, 1, 0)
        return n

    n = lax.fori_loop(0, slot_ref.shape[0] // 8, compact, 0)
    for k in range(STEP2):
        list_ref[n + k] = 8 << 10
    count_ref[0] = n
    rounds = pl.cdiv(n, STEP)

    def out_copy(i, k):
        side = lax.rem(i, 2)
        to = jnp.minimum(i * STEP + k, KEPT)
        return pltpu.make_async_copy(bufs[k].at[side], tiles_ref.at[to], sem.at[side, k])

    def step(i, carry):
        @pl.when(i >= 2)
        def _():
            for k in range(STEP):
                out_copy(i - 2, k).wait()

        side = lax.rem(i, 2)
        for k in range(STEP):
            t, held, b = decode(list_ref[i * STEP + k])
            build_tile(held, b, geo_ref, centre_ref, column_ref, offset_ref, bufs[k], side)
            add_product(t, block_of(flux_ref, b), bufs[k][side], sum_ref)
        for k in range(STEP):
            out_copy(i, k).start()
        return carry

    lax.fori_loop(0, rounds, step, 0)
    for back in (2, 1):

        @pl.when(rounds >= back)
        def _():
            for k in range(STEP):
                out_copy(rounds - back, k).wait()

    for u in range(16):
        lanes = slice(u * HALF, (u + 1) * HALF)
        radiosity = emission_ref[:, lanes] + reflect_ref[:, lanes] * sum_ref[u // 2, u % 2]
        leaving_ref[u] = (area_ref[:, lanes] * radiosity).astype(jnp.bfloat16)


def second_kernel(
    list_ref, count_ref, geo_ref, flux_ref, own_ref, emission_ref, reflect_ref, tiles_ref,
    out_ref,
    centre_ref, column_ref, offset_ref, sum_ref, spare_ref, buf_ref, sem,
):
    n = count_ref[0]
    sum_ref[...] = jnp.zeros_like(sum_ref)
    rounds = pl.cdiv(jnp.minimum(n, KEPT), STEP2)

    def in_copy(i):
        side = lax.rem(i, 2)
        return pltpu.make_async_copy(
            tiles_ref.at[pl.ds(i * STEP2, STEP2)], buf_ref.at[side], sem.at[side]
        )

    @pl.when(rounds > 0)
    def _():
        in_copy(0).start()

    def step(i, carry):
        @pl.when(i + 1 < rounds)
        def _():
            in_copy(i + 1).start()

        in_copy(i).wait()
        side = lax.rem(i, 2)
        for k in range(STEP2):
            t, held, b = decode(list_ref[i * STEP2 + k])
            add_product(t, block_of(flux_ref, b), buf_ref[side, k], sum_ref)
        return carry

    lax.fori_loop(0, rounds, step, 0)

    @pl.when(n > KEPT)
    def _():
        prepare_targets(own_ref, centre_ref, column_ref, offset_ref)

        def again(e, carry):
            t, held, b = decode(list_ref[e])
            build_tile(held, b, geo_ref, centre_ref, column_ref, offset_ref, spare_ref, 0)
            add_product(t, block_of(flux_ref, b), spare_ref[0], sum_ref)
            return carry

        lax.fori_loop(KEPT, n, again, 0)

    for u in range(16):
        lanes = slice(u * HALF, (u + 1) * HALF)
        out_ref[:, lanes] = emission_ref[:, lanes] + reflect_ref[:, lanes] * sum_ref[u // 2, u % 2]


def per_device(
    positions, normals, emission, material, area_level, reflect_table, area_table, pair_slots
):
    patches = positions.shape[1]
    units = patches // HALF
    me = lax.axis_index("gx") * lax.axis_size("gy") + lax.axis_index("gy")
    level_hot = (
        area_level[None, :] == jnp.arange(area_table.shape[0], dtype=jnp.int32)[:, None]
    ).astype(jnp.float32)
    area = jnp.sum(level_hot * area_table[:, None], axis=0)[None, :]
    kind_hot = (
        material[None, :] == jnp.arange(reflect_table.shape[0], dtype=jnp.int32)[:, None]
    ).astype(jnp.float32)
    reflect = jnp.dot(jnp.transpose(reflect_table), kind_hot, precision=lax.Precision.HIGHEST)

    def in_units(x):
        return jnp.transpose(x.reshape(x.shape[0], units, HALF), (1, 0, 2))

    row, column = pair_slots[0, :, :, 0], pair_slots[0, :, :, 1]
    full = row >= 0
    peers = row.shape[0]
    codes = jnp.where(full, row * 8 + column, -1).reshape(1, -1).astype(jnp.float32)
    codes = jnp.pad(codes, ((0, 0), (0, patches - codes.shape[1])))
    own_geo = in_units(jnp.concatenate([positions, area, normals, codes], axis=0))
    flux = in_units((area * emission).astype(jnp.bfloat16))
    geo, all_flux = gather_all([own_geo, flux], (GEO_PARTS, FLUX_PARTS), 0)
    blocks = peers * 8
    own_blocks = own_geo.reshape(8, 2, 8, HALF)
    at = me * 2
    served = lax.dynamic_slice(
        geo.reshape(peers, units, 8, HALF), (0, at // HALF, 7, at % HALF), (peers, 1, 1, 2)
    ).reshape(peers, 2).astype(jnp.int32)
    geo = geo.reshape(blocks, 2, 8, HALF)
    peer = jnp.arange(peers, dtype=jnp.int32)[:, None] * 8
    own_list = jnp.where(full, row * 1024 + peer + column, -1)
    served_list = jnp.where(served >= 0, (served % 8) * 1024 + peer + served // 8, -1)
    slots = jnp.concatenate([own_list.reshape(-1), served_list.reshape(-1)])

    vmem = pl.BlockSpec(memory_space=pltpu.VMEM)
    smem = pl.BlockSpec(memory_space=pltpu.SMEM)
    anywhere = pl.BlockSpec(memory_space=pl.ANY)
    scratch = [
        pltpu.VMEM((8, 8, BLK), jnp.float32),
        pltpu.VMEM((8, 3 * BLK, 64), jnp.bfloat16),
        pltpu.VMEM((8, BLK, HALF), jnp.float32),
        pltpu.VMEM((9, 2, BANDS, HALF), jnp.float32),
    ]
    limit = pltpu.CompilerParams(vmem_limit_bytes=48 << 20)
    leaving, tiles, listed, counted = pl.pallas_call(
        first_kernel,
        out_shape=[
            jax.ShapeDtypeStruct((units, BANDS, HALF), jnp.bfloat16),
            jax.ShapeDtypeStruct((KEPT + 8, BLK, BLK), jnp.bfloat16),
            jax.ShapeDtypeStruct((slots.shape[0] + STEP2,), jnp.int32),
            jax.ShapeDtypeStruct((1,), jnp.int32),
        ],
        in_specs=[smem] + [vmem] * 6,
        out_specs=[vmem, anywhere, smem, smem],
        scratch_shapes=scratch
        + [pltpu.VMEM((2, BLK, BLK), jnp.bfloat16)] * STEP
        + [pltpu.SemaphoreType.DMA((2, STEP))],
        compiler_params=limit,
        name="first_sweep",
    )(slots, geo, all_flux.reshape(blocks, 2, BANDS, HALF), own_blocks, emission, reflect, area)
    (all_flux,) = gather_all([leaving], (FLUX_PARTS,), 1)
    return pl.pallas_call(
        second_kernel,
        out_shape=jax.ShapeDtypeStruct((BANDS, patches), jnp.float32),
        in_specs=[smem, smem] + [vmem] * 5 + [anywhere],
        out_specs=vmem,
        scratch_shapes=scratch
        + [
            pltpu.VMEM((1, BLK, BLK), jnp.bfloat16),
            pltpu.VMEM((2, STEP2, BLK, BLK), jnp.bfloat16),
            pltpu.SemaphoreType.DMA((2,)),
        ],
        compiler_params=limit,
        name="second_sweep",
    )(
        listed, counted, geo, all_flux.reshape(blocks, 2, BANDS, HALF), own_blocks,
        emission, reflect, tiles,
    )


def solution(mesh):
    placed = (
        P(None, AXES),
        P(None, AXES),
        P(None, AXES),
        P(AXES),
        P(AXES),
        P(),
        P(),
        P(AXES, None, None, None),
    )
    return jax.shard_map(
        per_device, mesh=mesh, in_specs=placed, out_specs=P(None, AXES), check_vma=False
    )
```

```python
import functools
import math

import jax
import jax.numpy as jnp
from jax import lax
from jax.experimental import pallas as pl
from jax.experimental.pallas import tpu as pltpu
from jax.sharding import PartitionSpec as P

MESH = pl.DeviceIdType.MESH
BANDS = 16
BLK = 256
HALF = 128
ITERS = 2
AXES = ("gx", "gy")
SIDE = 4
ORDERS = (("x", "y", "z"), ("y", "z", "x"), ("z", "x", "y"))
FLUX_PARTS = (6, 5, 5)
GEO_PARTS = (5, 6, 5)
KEPT = 336
STEP = 8
STEP2 = 8
CHUNK = 64
DEPTH = 4
SKIP = 8 << 10
KAPPA = (math.pi - 1.0) / math.pi


def my_place():
    z = lax.axis_index("gx")
    inner = lax.axis_index("gy")
    place = {"z": z, "y": lax.div(inner, 2 * SIDE), "x": lax.rem(lax.div(inner, 2), SIDE)}
    return place, lax.rem(inner, 2)


def device_of(place, core):
    return (place["z"], (place["y"] * SIDE + place["x"]) * 2 + core)


def moved(place, axis, by):
    other = dict(place)
    other[axis] = lax.rem(place[axis] + (by + SIDE), SIDE)
    return other


def gather_kernel(parts, count, *refs):
    srcs, bufs = refs[:count], refs[count : 2 * count]
    send_sem, recv_sem, local_sem = refs[2 * count :]
    here, core = my_place()
    other_core = device_of(here, 1 - core)
    own_copies = []
    for b in range(count):
        place = bufs[b].at[here["z"], here["y"], here["x"], core]
        own_copies.append(pltpu.make_async_copy(srcs[b], place, local_sem.at[b]))
        own_copies[-1].start()
    barrier = pltpu.get_barrier_semaphore()
    peers = [device_of(moved(here, axis, by), core) for axis in "zyx" for by in (1, -1)]
    peers.append(other_core)
    for peer in peers:
        pl.semaphore_signal(barrier, inc=1, device_id=peer, device_id_type=MESH)
    pl.semaphore_wait(barrier, len(peers))
    started = []
    shared = []

    def send(src, dst, to):
        n = len(started)
        copy = pltpu.make_async_remote_copy(
            src_ref=src,
            dst_ref=dst,
            send_sem=send_sem.at[n],
            recv_sem=recv_sem.at[n],
            device_id=to,
            device_id_type=MESH,
        )
        copy.start()
        started.append(copy)
        return copy

    def view(b, index, first, size):
        return bufs[b].at[index["z"], index["y"], index["x"], core, pl.ds(first, size)]

    def share(b, index, first, size):
        piece = view(b, index, first, size)
        shared.append(send(piece, piece, other_core))

    work = []
    for b in range(count):
        first = 0
        for k, size in enumerate(parts[b]):
            work.append((b, k, first, size))
            first += size

    def group(phase, k, by):
        order = ORDERS[k]
        index = moved(here, order[phase], by)
        for axis in order[:phase]:
            index[axis] = pl.ds(0, SIDE)
        return index

    def half_of(phase, k, index, first, size, which):
        if phase == 0:
            low = (size + 1) // 2
            return (index, first, low) if which == 0 else (index, first + low, size - low)
        index = dict(index)
        index[ORDERS[k][0]] = pl.ds(2 * which, 2)
        return index, first, size

    for phase in range(3):
        up, down, up2, down2 = {}, {}, {}, {}
        for item in work:
            b, k, first, size = item
            axis = ORDERS[k][phase]
            dst = view(b, group(phase, k, 0), first, size)
            src = dst if phase else srcs[b].at[pl.ds(first, size)]
            up[item] = send(src, dst, device_of(moved(here, axis, 1), core))
            down[item] = send(src, dst, device_of(moved(here, axis, -1), core))
        if phase == 0:
            for b in range(count):
                place = bufs[b].at[here["z"], here["y"], here["x"], core]
                shared.append(send(srcs[b], place, other_core))
            for copy in own_copies:
                copy.wait()
        for item in work:
            b, k, first, size = item
            axis = ORDERS[k][phase]
            below, above = group(phase, k, -1), group(phase, k, 1)
            up[item].wait_recv()
            piece = view(b, *half_of(phase, k, below, first, size, 0))
            up2[item] = send(piece, piece, device_of(moved(here, axis, 1), core))
            down[item].wait_recv()
            piece = view(b, *half_of(phase, k, above, first, size, 1))
            down2[item] = send(piece, piece, device_of(moved(here, axis, -1), core))
            share(b, below, first, size)
            share(b, above, first, size)
        for item in work:
            b, k, first, size = item
            up2[item].wait_recv()
            down2[item].wait_recv()
            share(b, group(phase, k, 2), first, size)
    for copy in shared:
        copy.wait_recv()
    for copy in started:
        copy.wait_send()


def gather_all(arrays, parts, collective_id):
    count = len(arrays)
    copies = (3 * 7 * 3 + 1) * count
    anywhere = pl.BlockSpec(memory_space=pl.ANY)
    return pl.pallas_call(
        functools.partial(gather_kernel, parts, count),
        out_shape=[
            jax.ShapeDtypeStruct((SIDE, SIDE, SIDE, 2) + a.shape, a.dtype) for a in arrays
        ],
        in_specs=[anywhere] * count,
        out_specs=[anywhere] * count,
        scratch_shapes=[
            pltpu.SemaphoreType.DMA((copies,)),
            pltpu.SemaphoreType.DMA((copies,)),
            pltpu.SemaphoreType.DMA((count,)),
        ],
        compiler_params=pltpu.CompilerParams(collective_id=collective_id, has_side_effects=True),
        name="gather_all",
    )(*arrays)


def split3(x):
    a = x.astype(jnp.bfloat16).astype(jnp.float32)
    rest = x - a
    b = rest.astype(jnp.bfloat16).astype(jnp.float32)
    return a, b, rest - b


def block_of(ref, b):
    return jnp.concatenate([ref[b, 0], ref[b, 1]], axis=1)


def centred(rows, centre):
    moved_rows = rows - centre
    squares = moved_rows * moved_rows
    cross = moved_rows * pltpu.roll(moved_rows, 4, 0)
    reach = (squares[0:1] + squares[1:2] + squares[2:3]) + 0.5 * rows[3:4]
    plane = -(cross[0:1] + cross[1:2] + cross[2:3])
    return moved_rows, reach, plane


def source_rows(rows, centre):
    at = lax.broadcasted_iota(jnp.int32, rows.shape, 0)
    base, reach, plane = centred(rows, centre)
    base = jnp.where(at == 3, reach, jnp.where(at == 7, plane, base))
    a, b, c = split3(base)
    one = jnp.where(at < 3, 1.0, 0.0)
    stacked = jnp.concatenate([a, a, a, b, b, c, one, jnp.zeros_like(one)], axis=0)
    return stacked.astype(jnp.bfloat16), (KAPPA * 0.5) * rows[3:4]


def target_columns(rows, centre):
    at = lax.broadcasted_iota(jnp.int32, rows.shape, 0)
    base, reach, plane = centred(rows, centre)
    zero = jnp.zeros_like(base)
    swapped = pltpu.roll(base, 4, 0)
    facing = jnp.where(at < 3, swapped, 0.0) * (1.0 / math.pi)
    seen = jnp.where((at >= 4) & (at < 7), swapped, jnp.where(at == 7, 1.0, 0.0))
    spread = jnp.where(at < 3, -2.0 * base, jnp.where(at == 3, 1.0, 0.0))
    columns = []
    for factor, constant in ((facing, plane * (1.0 / math.pi)), (seen, None), (spread, reach)):
        a, b, c = split3(factor)
        last = zero
        if constant is not None:
            d, e, f = split3(constant)
            last = jnp.where(at == 0, d, jnp.where(at == 1, e, jnp.where(at == 2, f, 0.0)))
        stacked = jnp.concatenate([a, b, c, a, b, a, last, zero], axis=0)
        columns.append(jnp.transpose(stacked).astype(jnp.bfloat16))
    return columns, (KAPPA * 0.5) * rows[3:4]


def prepare_targets(own_ref, centre_ref, column_ref, offset_ref):
    for t in range(8):
        rows = block_of(own_ref, t)
        at = lax.broadcasted_iota(jnp.int32, rows.shape, 0)
        centre = jnp.where(at < 3, jnp.broadcast_to(rows[:, 0:1], rows.shape), 0.0)
        centre_ref[t] = centre
        columns, offset = target_columns(rows, centre)
        for r in range(0, BLK, CHUNK):
            column_ref[t, 3 * r : 3 * (r + CHUNK)] = jnp.concatenate(
                [c[r : r + CHUNK] for c in columns], axis=0
            )
        offset_ref[t] = jnp.transpose(jnp.broadcast_to(offset, (HALF, BLK)))


def build_tile(t, b, geo_ref, centre_ref, column_ref, offset_ref, tile_ref, slot):
    source, source_offset = source_rows(block_of(geo_ref, b), centre_ref[t])
    for r in range(0, BLK, CHUNK):
        terms = jnp.dot(
            column_ref[t, 3 * r : 3 * (r + CHUNK), :], source, preferred_element_type=jnp.float32
        )
        facing, seen, spread = terms[:CHUNK], terms[CHUNK : 2 * CHUNK], terms[2 * CHUNK :]
        offset = offset_ref[t, r : r + CHUNK, :]
        offset = jnp.concatenate([offset, offset], axis=1)
        over = jnp.maximum(facing, 0.0) * jnp.maximum(seen, 0.0)
        under = spread * ((spread - offset) - source_offset)
        inverse = pl.reciprocal(under, approx=True)
        inverse = inverse * (2.0 - under * inverse)
        tile_ref[slot, r : r + CHUNK, :] = (over * inverse).astype(jnp.bfloat16)


def add_product(t, flux, tile, sum_ref):
    term = lax.dot_general(
        flux, tile, (((1,), (1,)), ((), ())), preferred_element_type=jnp.float32
    )
    sum_ref[t, 0] += term[:, :HALF]
    sum_ref[t, 1] += term[:, HALF:]


def decode(code):
    t = lax.shift_right_logical(code, 10)
    return t, jnp.minimum(t, 7), lax.bitwise_and(code, 1023)


def first_kernel(
    slot_ref, geo_all, flux_all, own_ref, emission_ref, reflect_ref, area_ref,
    leaving_ref, tiles_ref, list_ref, count_ref,
    geo_ref, flux_ref, load_sem, centre_ref, column_ref, offset_ref, sum_ref, *rest,
):
    bufs, sem = rest[:STEP], rest[STEP]
    loads = [
        pltpu.make_async_copy(geo_all, geo_ref, load_sem.at[0]),
        pltpu.make_async_copy(flux_all, flux_ref, load_sem.at[1]),
    ]
    for load in loads:
        load.start()
    prepare_targets(own_ref, centre_ref, column_ref, offset_ref)
    sum_ref[...] = jnp.zeros_like(sum_ref)
    bufs[-1][1] = jnp.zeros_like(bufs[-1][1])

    def compact(e, n):
        for k in range(8):
            code = slot_ref[e * 8 + k]
            list_ref[n] = code
            n = n + jnp.where(code >= 0, 1, 0)
        return n

    n = lax.fori_loop(0, slot_ref.shape[0] // 8, compact, 0)
    for k in range(STEP2):
        list_ref[n + k] = SKIP
    count_ref[0] = n
    rounds = pl.cdiv(n, STEP)
    for load in loads:
        load.wait()

    def out_copy(i, k):
        side = lax.rem(i, 2)
        to = jnp.minimum(i * STEP + k, KEPT)
        return pltpu.make_async_copy(bufs[k].at[side], tiles_ref.at[to], sem.at[side, k])

    def add_tile(code, k, side):
        t, held, b = decode(code)
        add_product(t, block_of(flux_ref, b), bufs[k][side], sum_ref)

    def step(i, carry):
        @pl.when(i >= 2)
        def _():
            for k in range(STEP):
                out_copy(i - 2, k).wait()

        side = lax.rem(i, 2)
        before = jnp.where(i > 0, list_ref[jnp.maximum(i * STEP - 1, 0)], SKIP)
        for k in range(STEP):
            code = list_ref[i * STEP + k]
            t, held, b = decode(code)
            build_tile(held, b, geo_ref, centre_ref, column_ref, offset_ref, bufs[k], side)
            if k == 0:
                add_tile(before, STEP - 1, 1 - side)
            else:
                add_tile(before, k - 1, side)
            before = code
        for k in range(STEP):
            out_copy(i, k).start()
        return carry

    lax.fori_loop(0, rounds, step, 0)
    last = jnp.where(rounds > 0, list_ref[jnp.maximum(rounds * STEP - 1, 0)], SKIP)
    add_tile(last, STEP - 1, lax.rem(rounds + 1, 2))
    for back in (2, 1):

        @pl.when(rounds >= back)
        def _():
            for k in range(STEP):
                out_copy(rounds - back, k).wait()

    for u in range(16):
        lanes = slice(u * HALF, (u + 1) * HALF)
        radiosity = emission_ref[:, lanes] + reflect_ref[:, lanes] * sum_ref[u // 2, u % 2]
        leaving_ref[u] = (area_ref[:, lanes] * radiosity).astype(jnp.bfloat16)


def second_kernel(
    list_ref, count_ref, geo_all, flux_all, own_ref, emission_ref, reflect_ref, tiles_ref,
    out_ref,
    geo_ref, flux_ref, load_sem, centre_ref, column_ref, offset_ref, sum_ref, spare_ref, buf_ref, sem,
):
    n = count_ref[0]
    rounds = pl.cdiv(jnp.minimum(n, KEPT), STEP2)

    def in_copy(i):
        side = lax.rem(i, DEPTH)
        return pltpu.make_async_copy(
            tiles_ref.at[pl.ds(i * STEP2, STEP2)], buf_ref.at[side], sem.at[side]
        )

    load = pltpu.make_async_copy(flux_all, flux_ref, load_sem.at[1])
    load.start()
    for i in range(DEPTH - 1):

        @pl.when(i < rounds)
        def _():
            in_copy(i).start()

    sum_ref[...] = jnp.zeros_like(sum_ref)
    load.wait()

    def step(i, carry):
        @pl.when(i + DEPTH - 1 < rounds)
        def _():
            in_copy(i + DEPTH - 1).start()

        in_copy(i).wait()
        side = lax.rem(i, DEPTH)
        for k in range(STEP2):
            t, held, b = decode(list_ref[i * STEP2 + k])
            add_product(t, block_of(flux_ref, b), buf_ref[side, k], sum_ref)
        return carry

    lax.fori_loop(0, rounds, step, 0)

    @pl.when(n > KEPT)
    def _():
        again_load = pltpu.make_async_copy(geo_all, geo_ref, load_sem.at[0])
        again_load.start()
        again_load.wait()
        prepare_targets(own_ref, centre_ref, column_ref, offset_ref)

        def again(e, carry):
            t, held, b = decode(list_ref[e])
            build_tile(held, b, geo_ref, centre_ref, column_ref, offset_ref, spare_ref, 0)
            add_product(t, block_of(flux_ref, b), spare_ref[0], sum_ref)
            return carry

        lax.fori_loop(KEPT, n, again, 0)

    for u in range(16):
        lanes = slice(u * HALF, (u + 1) * HALF)
        out_ref[:, lanes] = emission_ref[:, lanes] + reflect_ref[:, lanes] * sum_ref[u // 2, u % 2]


def per_device(
    positions, normals, emission, material, area_level, reflect_table, area_table, pair_slots
):
    patches = positions.shape[1]
    units = patches // HALF
    me = lax.axis_index("gx") * lax.axis_size("gy") + lax.axis_index("gy")
    level_hot = (
        area_level[None, :] == jnp.arange(area_table.shape[0], dtype=jnp.int32)[:, None]
    ).astype(jnp.float32)
    area = jnp.sum(level_hot * area_table[:, None], axis=0)[None, :]
    kind_hot = (
        material[None, :] == jnp.arange(reflect_table.shape[0], dtype=jnp.int32)[:, None]
    ).astype(jnp.float32)
    reflect = jnp.dot(jnp.transpose(reflect_table), kind_hot, precision=lax.Precision.HIGHEST)

    def in_units(x):
        return jnp.transpose(x.reshape(x.shape[0], units, HALF), (1, 0, 2))

    row, column = pair_slots[0, :, :, 0], pair_slots[0, :, :, 1]
    full = row >= 0
    peers = row.shape[0]
    codes = jnp.where(full, row * 8 + column, -1).reshape(1, -1).astype(jnp.float32)
    codes = jnp.pad(codes, ((0, 0), (0, patches - codes.shape[1])))
    own_geo = in_units(jnp.concatenate([positions, area, normals, codes], axis=0))
    flux = in_units((area * emission).astype(jnp.bfloat16))
    geo, all_flux = gather_all([own_geo, flux], (GEO_PARTS, FLUX_PARTS), 0)
    blocks = peers * 8
    own_blocks = own_geo.reshape(8, 2, 8, HALF)
    at = me * 2
    served = lax.dynamic_slice(
        geo.reshape(peers, units, 8, HALF), (0, at // HALF, 7, at % HALF), (peers, 1, 1, 2)
    ).reshape(peers, 2).astype(jnp.int32)
    geo = geo.reshape(blocks, 2, 8, HALF)
    peer = jnp.arange(peers, dtype=jnp.int32)[:, None] * 8
    own_list = jnp.where(full, row * 1024 + peer + column, -1)
    served_list = jnp.where(served >= 0, (served % 8) * 1024 + peer + served // 8, -1)
    slots = jnp.concatenate([own_list.reshape(-1), served_list.reshape(-1)])

    vmem = pl.BlockSpec(memory_space=pltpu.VMEM)
    smem = pl.BlockSpec(memory_space=pltpu.SMEM)
    anywhere = pl.BlockSpec(memory_space=pl.ANY)
    scratch = [
        pltpu.VMEM((blocks, 2, 8, HALF), jnp.float32),
        pltpu.VMEM((blocks, 2, BANDS, HALF), jnp.bfloat16),
        pltpu.SemaphoreType.DMA((2,)),
        pltpu.VMEM((8, 8, BLK), jnp.float32),
        pltpu.VMEM((8, 3 * BLK, 64), jnp.bfloat16),
        pltpu.VMEM((8, BLK, HALF), jnp.float32),
        pltpu.VMEM((9, 2, BANDS, HALF), jnp.float32),
    ]
    limit = pltpu.CompilerParams(vmem_limit_bytes=48 << 20)
    leaving, tiles, listed, counted = pl.pallas_call(
        first_kernel,
        out_shape=[
            jax.ShapeDtypeStruct((units, BANDS, HALF), jnp.bfloat16),
            jax.ShapeDtypeStruct((KEPT + 8, BLK, BLK), jnp.bfloat16),
            jax.ShapeDtypeStruct((slots.shape[0] + STEP2,), jnp.int32),
            jax.ShapeDtypeStruct((1,), jnp.int32),
        ],
        in_specs=[smem, anywhere, anywhere] + [vmem] * 4,
        out_specs=[vmem, anywhere, smem, smem],
        scratch_shapes=scratch
        + [pltpu.VMEM((2, BLK, BLK), jnp.bfloat16)] * STEP
        + [pltpu.SemaphoreType.DMA((2, STEP))],
        compiler_params=limit,
        name="first_sweep",
    )(slots, geo, all_flux.reshape(blocks, 2, BANDS, HALF), own_blocks, emission, reflect, area)
    (all_flux,) = gather_all([leaving], (FLUX_PARTS,), 1)
    return pl.pallas_call(
        second_kernel,
        out_shape=jax.ShapeDtypeStruct((BANDS, patches), jnp.float32),
        in_specs=[smem, smem, anywhere, anywhere] + [vmem] * 3 + [anywhere],
        out_specs=vmem,
        scratch_shapes=scratch
        + [
            pltpu.VMEM((1, BLK, BLK), jnp.bfloat16),
            pltpu.VMEM((DEPTH, STEP2, BLK, BLK), jnp.bfloat16),
            pltpu.SemaphoreType.DMA((DEPTH,)),
        ],
        compiler_params=limit,
        name="second_sweep",
    )(
        listed, counted, geo, all_flux.reshape(blocks, 2, BANDS, HALF), own_blocks,
        emission, reflect, tiles,
    )


def solution(mesh):
    placed = (
        P(None, AXES),
        P(None, AXES),
        P(None, AXES),
        P(AXES),
        P(AXES),
        P(),
        P(),
        P(AXES, None, None, None),
    )
    return jax.shard_map(
        per_device, mesh=mesh, in_specs=placed, out_specs=P(None, AXES), check_vma=False
    )
```

```python
import functools
import math

import jax
import jax.numpy as jnp
from jax import lax
from jax.experimental import pallas as pl
from jax.experimental.pallas import tpu as pltpu
from jax.sharding import PartitionSpec as P

MESH = pl.DeviceIdType.MESH
BANDS = 16
BLK = 256
HALF = 128
ITERS = 2
AXES = ("gx", "gy")
SIDE = 4
ORDERS = (("x", "y", "z"), ("y", "z", "x"), ("z", "x", "y"))
FIRST_PARTS = (((0, 11), (1, 5)), ((1, 6), (2, 10)))
LATER_PARTS = (((0, 6), (1, 5), (2, 5)),)
KEPT = 336
STEP = 8
STEP2 = 8
CHUNK = 64
DEPTH = 4
SKIP = 8 << 10
KAPPA = (math.pi - 1.0) / math.pi


def my_place():
    z = lax.axis_index("gx")
    inner = lax.axis_index("gy")
    place = {"z": z, "y": lax.div(inner, 2 * SIDE), "x": lax.rem(lax.div(inner, 2), SIDE)}
    return place, lax.rem(inner, 2)


def device_of(place, core):
    return (place["z"], (place["y"] * SIDE + place["x"]) * 2 + core)


def moved(place, axis, by):
    other = dict(place)
    other[axis] = lax.rem(place[axis] + (by + SIDE), SIDE)
    return other


def own_first(refs, srcs):
    position_ref, normal_ref, emission_ref, level_ref, area_ref, slot_ref = refs
    geo_ref, flux_ref = srcs
    for u in range(position_ref.shape[1] // HALF):
        lanes = slice(u * HALF, (u + 1) * HALF)
        level = level_ref[:, lanes]
        area = jnp.zeros(level.shape, jnp.float32)
        for m in range(area_ref.shape[0]):
            area = jnp.where(level == m, area_ref[m], area)
        code = jnp.zeros(area.shape, jnp.float32)
        if u < 2:
            row, column = slot_ref[u, 0:1, :], slot_ref[u, 1:2, :]
            code = jnp.where(row >= 0, row * 8 + column, -1).astype(jnp.float32)
        geo_ref[u] = jnp.concatenate(
            [position_ref[:, lanes], area, normal_ref[:, lanes], code], axis=0
        )
        flux_ref[u] = (area * emission_ref[:, lanes]).astype(jnp.bfloat16)


def gather_kernel(parts, count, prologue, inputs, *refs):
    bufs, rest = refs[inputs : inputs + count], refs[inputs + count :]
    send_sem, recv_sem, local_sem = rest[:3]
    srcs = rest[3:] if prologue else refs[:count]
    here, core = my_place()
    other_core = device_of(here, 1 - core)
    barrier = pltpu.get_barrier_semaphore()
    peers = [device_of(moved(here, axis, by), core) for axis in "zyx" for by in (1, -1, 2)]
    peers.append(other_core)
    for peer in peers:
        pl.semaphore_signal(barrier, inc=1, device_id=peer, device_id_type=MESH)
    if prologue:
        prologue(refs[:inputs], srcs)
    own_copies = []
    for b in range(count):
        place = bufs[b].at[here["z"], here["y"], here["x"], core]
        own_copies.append(pltpu.make_async_copy(srcs[b], place, local_sem.at[b]))
        own_copies[-1].start()
    pl.semaphore_wait(barrier, len(peers))
    started = []
    shared = []

    def send(src, dst, to):
        n = len(started)
        copy = pltpu.make_async_remote_copy(
            src_ref=src,
            dst_ref=dst,
            send_sem=send_sem.at[n],
            recv_sem=recv_sem.at[n],
            device_id=to,
            device_id_type=MESH,
        )
        copy.start()
        started.append(copy)
        return copy

    def view(b, index, first, size):
        return bufs[b].at[index["z"], index["y"], index["x"], core, pl.ds(first, size)]

    def share(b, index, first, size):
        piece = view(b, index, first, size)
        shared.append(send(piece, piece, other_core))

    work = []
    for b in range(count):
        first = 0
        for k, size in parts[b]:
            work.append((b, k, first, size))
            first += size

    for copy in own_copies:
        copy.wait()

    def at(k, line, plane, far):
        index = {}
        for axis, by in zip(ORDERS[k], (line, plane, far)):
            index[axis] = pl.ds(0, SIDE) if by is None else moved(here, axis, by)[axis]
        return index

    def to(k, stage, by):
        return device_of(moved(here, ORDERS[k][stage], by), core)

    def pass_on(item, stage, by, index):
        b, k, first, size = item
        piece = view(b, index, first, size)
        return send(piece, piece, to(k, stage, by))

    def half(k, index, which):
        index = dict(index)
        index[ORDERS[k][0]] = pl.ds(2 * which, 2)
        return index

    line, plane, ahead, far, again = {}, {}, {}, {}, {}
    for item in work:
        b, k, first, size = item
        src, dst = srcs[b].at[pl.ds(first, size)], view(b, here, first, size)
        line[item] = [send(src, dst, to(k, 0, by)) for by in (1, -1, 2)]
    for item in work:
        b, k, first, size = item
        for copy in line[item]:
            copy.wait_recv()
        mine = at(k, None, 0, 0)
        plane[item] = {by: pass_on(item, 1, by, mine) for by in (1, -1)}
        for by in (1, -1):
            far[item, 0, by] = pass_on(item, 2, by, mine)
        share(b, mine, first, size)
    for item in work:
        b, k, first, size = item
        plane[item][1].wait_recv()
        up = pass_on(item, 1, 1, half(k, at(k, None, -1, 0), 0))
        plane[item][-1].wait_recv()
        down = pass_on(item, 1, -1, half(k, at(k, None, 1, 0), 1))
        ahead[item] = [up, down]
        for row in (-1, 1):
            index = at(k, None, row, 0)
            for by in (1, -1):
                far[item, row, by] = pass_on(item, 2, by, index)
            share(b, index, first, size)

    def forward(item, row):
        k = item[1]
        far[item, row, 1].wait_recv()
        up = pass_on(item, 2, 1, half(k, at(k, None, row, -1), 0))
        far[item, row, -1].wait_recv()
        down = pass_on(item, 2, -1, half(k, at(k, None, row, 1), 1))
        again[item, row] = [up, down]

    def share_far(item, row):
        b, k, first, size = item
        share(b, at(k, None, row, -1), first, size)
        share(b, at(k, None, row, 1), first, size)

    for item in work:
        forward(item, 0)
        share_far(item, 0)
    for item in work:
        b, k, first, size = item
        for copy in ahead[item]:
            copy.wait_recv()
        index = at(k, None, 2, 0)
        for by in (1, -1):
            far[item, 2, by] = pass_on(item, 2, by, index)
        share(b, index, first, size)
    for row in (-1, 1, 2):
        for item in work:
            forward(item, row)
            share_far(item, row)
    for row in (0, -1, 1, 2):
        for item in work:
            b, k, first, size = item
            for copy in again[item, row]:
                copy.wait_recv()
            if row == 1:
                pass
            share(b, at(k, None, row, 2), first, size)
    for copy in shared:
        copy.wait_recv()
    for copy in started:
        copy.wait_send()


def gather_all(shapes, parts, collective_id, specs, inputs, prologue=None):
    count = len(shapes)
    copies = 39 * sum(len(p) for p in parts)
    own = [pltpu.VMEM(a.shape, a.dtype) for a in shapes] if prologue else []
    return pl.pallas_call(
        functools.partial(gather_kernel, parts, count, prologue, len(inputs)),
        out_shape=[
            jax.ShapeDtypeStruct((SIDE, SIDE, SIDE, 2) + a.shape, a.dtype) for a in shapes
        ],
        in_specs=specs,
        out_specs=[pl.BlockSpec(memory_space=pl.ANY)] * count,
        scratch_shapes=[
            pltpu.SemaphoreType.DMA((copies,)),
            pltpu.SemaphoreType.DMA((copies,)),
            pltpu.SemaphoreType.DMA((count,)),
        ]
        + own,
        compiler_params=pltpu.CompilerParams(
            collective_id=collective_id, has_side_effects=True, vmem_limit_bytes=2 << 20
        ),
        name="gather_all",
    )(*inputs)


def my_block():
    return (lax.axis_index("gx") * lax.axis_size("gy") + lax.axis_index("gy")) * 8


def reflect_of(table_ref, material_ref, lanes):
    material = material_ref[:, lanes]
    kinds = table_ref.shape[0]
    hot = lax.broadcasted_iota(jnp.int32, (kinds, HALF), 0) == material
    return lax.dot_general(
        table_ref[...],
        jnp.where(hot, 1.0, 0.0),
        (((0,), (0,)), ((), ())),
        precision=lax.Precision.HIGHEST,
        preferred_element_type=jnp.float32,
    )


def split3(x):
    a = x.astype(jnp.bfloat16).astype(jnp.float32)
    rest = x - a
    b = rest.astype(jnp.bfloat16).astype(jnp.float32)
    return a, b, rest - b


def block_of(ref, b):
    return jnp.concatenate([ref[b, 0], ref[b, 1]], axis=1)


def centred(rows, centre):
    moved_rows = rows - centre
    squares = moved_rows * moved_rows
    cross = moved_rows * pltpu.roll(moved_rows, 4, 0)
    reach = (squares[0:1] + squares[1:2] + squares[2:3]) + 0.5 * rows[3:4]
    plane = -(cross[0:1] + cross[1:2] + cross[2:3])
    return moved_rows, reach, plane


def source_rows(rows, centre):
    at = lax.broadcasted_iota(jnp.int32, rows.shape, 0)
    base, reach, plane = centred(rows, centre)
    base = jnp.where(at == 3, reach, jnp.where(at == 7, plane, base))
    a, b, c = split3(base)
    one = jnp.where(at < 3, 1.0, 0.0)
    stacked = jnp.concatenate([a, a, a, b, b, c, one, jnp.zeros_like(one)], axis=0)
    return stacked.astype(jnp.bfloat16), (KAPPA * 0.5) * rows[3:4]


def target_columns(rows, centre):
    at = lax.broadcasted_iota(jnp.int32, rows.shape, 0)
    base, reach, plane = centred(rows, centre)
    zero = jnp.zeros_like(base)
    swapped = pltpu.roll(base, 4, 0)
    facing = jnp.where(at < 3, swapped, 0.0) * (1.0 / math.pi)
    seen = jnp.where((at >= 4) & (at < 7), swapped, jnp.where(at == 7, 1.0, 0.0))
    spread = jnp.where(at < 3, -2.0 * base, jnp.where(at == 3, 1.0, 0.0))
    columns = []
    for factor, constant in ((facing, plane * (1.0 / math.pi)), (seen, None), (spread, reach)):
        a, b, c = split3(factor)
        last = zero
        if constant is not None:
            d, e, f = split3(constant)
            last = jnp.where(at == 0, d, jnp.where(at == 1, e, jnp.where(at == 2, f, 0.0)))
        stacked = jnp.concatenate([a, b, c, a, b, a, last, zero], axis=0)
        columns.append(jnp.transpose(stacked).astype(jnp.bfloat16))
    return columns, (KAPPA * 0.5) * rows[3:4]


def prepare_targets(geo_ref, centre_ref, column_ref, offset_ref):
    for t in range(8):
        rows = block_of(geo_ref, my_block() + t)
        at = lax.broadcasted_iota(jnp.int32, rows.shape, 0)
        centre = jnp.where(at < 3, jnp.broadcast_to(rows[:, 0:1], rows.shape), 0.0)
        centre_ref[t] = centre
        columns, offset = target_columns(rows, centre)
        for r in range(0, BLK, CHUNK):
            column_ref[t, 3 * r : 3 * (r + CHUNK)] = jnp.concatenate(
                [c[r : r + CHUNK] for c in columns], axis=0
            )
        offset_ref[t] = jnp.transpose(jnp.broadcast_to(offset, (HALF, BLK)))


def build_tile(t, b, geo_ref, centre_ref, column_ref, offset_ref, tile_ref, slot):
    source, source_offset = source_rows(block_of(geo_ref, b), centre_ref[t])
    for r in range(0, BLK, CHUNK):
        terms = jnp.dot(
            column_ref[t, 3 * r : 3 * (r + CHUNK), :], source, preferred_element_type=jnp.float32
        )
        facing, seen, spread = terms[:CHUNK], terms[CHUNK : 2 * CHUNK], terms[2 * CHUNK :]
        offset = offset_ref[t, r : r + CHUNK, :]
        offset = jnp.concatenate([offset, offset], axis=1)
        over = jnp.maximum(facing, 0.0) * jnp.maximum(seen, 0.0)
        under = spread * ((spread - offset) - source_offset)
        inverse = pl.reciprocal(under, approx=True)
        inverse = inverse * (2.0 - under * inverse)
        tile_ref[slot, r : r + CHUNK, :] = (over * inverse).astype(jnp.bfloat16)


def add_product(t, flux, tile, sum_ref):
    term = lax.dot_general(
        flux, tile, (((1,), (1,)), ((), ())), preferred_element_type=jnp.float32
    )
    sum_ref[t, 0] += term[:, :HALF]
    sum_ref[t, 1] += term[:, HALF:]


def decode(code):
    t = lax.shift_right_logical(code, 10)
    return t, jnp.minimum(t, 7), lax.bitwise_and(code, 1023)


def first_kernel(
    geo_ref, flux_ref, emission_ref, material_ref, table_ref,
    leaving_ref, tiles_ref, list_ref, count_ref, kept_ref,
    code_ref, entry_ref, slot_ref, slot_sem, centre_ref, column_ref, offset_ref, sum_ref, *rest,
):
    bufs, sem = rest[:STEP], rest[STEP]
    first = my_block()
    peers = geo_ref.shape[0] // 8
    peer = lax.broadcasted_iota(jnp.int32, (1, peers), 1)
    at_me = lax.broadcasted_iota(jnp.int32, (8, HALF), 1) == lax.div(first, 8)
    pick = jnp.where(at_me, 1.0, 0.0).astype(jnp.bfloat16)
    entry_ref[...] = jnp.full_like(entry_ref, -1)
    for c in range(2):
        for p in range(peers):
            code_ref[p : p + 1, :] = geo_ref[p * 8, c, 7:8, :]
        served = lax.dot_general(
            pick,
            code_ref[...].astype(jnp.bfloat16),
            (((1,), (1,)), ((), ())),
            preferred_element_type=jnp.float32,
        )[0:1].astype(jnp.int32)
        owned = geo_ref[first, c, 7:8, :].astype(jnp.int32)
        for row, code, own in ((c, owned, True), (2 + c, served, False)):
            high, low = lax.shift_right_arithmetic(code, 3), lax.bitwise_and(code, 7)
            target, source = (high, low) if own else (low, high)
            entry_ref[row : row + 1, :] = jnp.where(
                code >= 0, target * 1024 + peer * 8 + source, -1
            )
    slot_copy = pltpu.make_async_copy(entry_ref, slot_ref, slot_sem)
    slot_copy.start()
    prepare_targets(geo_ref, centre_ref, column_ref, offset_ref)
    sum_ref[...] = jnp.zeros_like(sum_ref)
    slot_copy.wait()
    bufs[-1][1] = jnp.zeros_like(bufs[-1][1])

    def compact(e, n):
        for k in range(8):
            code = slot_ref[lax.div(e, HALF // 8), lax.rem(e, HALF // 8) * 8 + k]
            list_ref[n] = code
            n = n + jnp.where(code >= 0, 1, 0)
        return n

    n = lax.fori_loop(0, 4 * HALF // 8, compact, 0)
    for k in range(STEP2):
        list_ref[n + k] = SKIP
    count_ref[0] = n

    @pl.when(n > KEPT)
    def _():
        keep = pltpu.make_async_copy(geo_ref, kept_ref, slot_sem)
        keep.start()
        keep.wait()

    rounds = pl.cdiv(n, STEP)

    def out_copy(i, k):
        side = lax.rem(i, 2)
        to = jnp.minimum(i * STEP + k, KEPT)
        return pltpu.make_async_copy(bufs[k].at[side], tiles_ref.at[to], sem.at[side, k])

    def add_tile(code, k, side):
        t, held, b = decode(code)
        add_product(t, block_of(flux_ref, b), bufs[k][side], sum_ref)

    def step(i, carry):
        @pl.when(i >= 2)
        def _():
            for k in range(STEP):
                out_copy(i - 2, k).wait()

        side = lax.rem(i, 2)
        before = jnp.where(i > 0, list_ref[jnp.maximum(i * STEP - 1, 0)], SKIP)
        for k in range(STEP):
            code = list_ref[i * STEP + k]
            t, held, b = decode(code)
            build_tile(held, b, geo_ref, centre_ref, column_ref, offset_ref, bufs[k], side)
            if k == 0:
                add_tile(before, STEP - 1, 1 - side)
            else:
                add_tile(before, k - 1, side)
            before = code
        for k in range(STEP):
            out_copy(i, k).start()
        return carry

    lax.fori_loop(0, rounds, step, 0)
    last = jnp.where(rounds > 0, list_ref[jnp.maximum(rounds * STEP - 1, 0)], SKIP)
    add_tile(last, STEP - 1, lax.rem(rounds + 1, 2))
    for back in (2, 1):

        @pl.when(rounds >= back)
        def _():
            for k in range(STEP):
                out_copy(rounds - back, k).wait()

    for u in range(16):
        lanes = slice(u * HALF, (u + 1) * HALF)
        reflect = reflect_of(table_ref, material_ref, lanes)
        radiosity = emission_ref[:, lanes] + reflect * sum_ref[u // 2, u % 2]
        area = geo_ref[first + u // 2, u % 2, 3:4, :]
        leaving_ref[u] = (area * radiosity).astype(jnp.bfloat16)


def second_kernel(
    list_ref, count_ref, geo_all, flux_ref, emission_ref, material_ref, table_ref, tiles_ref,
    out_ref,
    geo_ref, load_sem, centre_ref, column_ref, offset_ref, sum_ref, spare_ref, buf_ref, sem,
):
    n = count_ref[0]
    rounds = pl.cdiv(jnp.minimum(n, KEPT), STEP2)

    def in_copy(i):
        side = lax.rem(i, DEPTH)
        return pltpu.make_async_copy(
            tiles_ref.at[pl.ds(i * STEP2, STEP2)], buf_ref.at[side], sem.at[side]
        )

    for i in range(DEPTH - 1):

        @pl.when(i < rounds)
        def _():
            in_copy(i).start()

    sum_ref[...] = jnp.zeros_like(sum_ref)

    def step(i, carry):
        @pl.when(i + DEPTH - 1 < rounds)
        def _():
            in_copy(i + DEPTH - 1).start()

        in_copy(i).wait()
        side = lax.rem(i, DEPTH)
        for k in range(STEP2):
            t, held, b = decode(list_ref[i * STEP2 + k])
            add_product(t, block_of(flux_ref, b), buf_ref[side, k], sum_ref)
        return carry

    lax.fori_loop(0, rounds, step, 0)

    @pl.when(n > KEPT)
    def _():
        again_load = pltpu.make_async_copy(geo_all, geo_ref, load_sem)
        again_load.start()
        again_load.wait()
        prepare_targets(geo_ref, centre_ref, column_ref, offset_ref)

        def again(e, carry):
            t, held, b = decode(list_ref[e])
            build_tile(held, b, geo_ref, centre_ref, column_ref, offset_ref, spare_ref, 0)
            add_product(t, block_of(flux_ref, b), spare_ref[0], sum_ref)
            return carry

        lax.fori_loop(KEPT, n, again, 0)

    for u in range(16):
        lanes = slice(u * HALF, (u + 1) * HALF)
        reflect = reflect_of(table_ref, material_ref, lanes)
        out_ref[:, lanes] = emission_ref[:, lanes] + reflect * sum_ref[u // 2, u % 2]


def per_device(
    positions, normals, emission, material, area_level, reflect_table, area_table, pair_slots
):
    patches = positions.shape[1]
    units = patches // HALF
    peers = pair_slots.shape[1]
    blocks = peers * 8
    vmem = pl.BlockSpec(memory_space=pltpu.VMEM)
    smem = pl.BlockSpec(memory_space=pltpu.SMEM)
    anywhere = pl.BlockSpec(memory_space=pl.ANY)
    material, level = material.reshape(1, patches), area_level.reshape(1, patches)
    slots = jnp.transpose(pair_slots[0], (1, 2, 0))
    geo_units = jax.ShapeDtypeStruct((units, 8, HALF), jnp.float32)
    flux_units = jax.ShapeDtypeStruct((units, BANDS, HALF), jnp.bfloat16)
    geo, flux = gather_all(
        [geo_units, flux_units],
        FIRST_PARTS,
        0,
        [vmem] * 4 + [smem, vmem],
        [positions, normals, emission, level, area_table, slots],
        own_first,
    )
    geo = geo.reshape(blocks, 2, 8, HALF)

    scratch = [
        pltpu.VMEM((8, 8, BLK), jnp.float32),
        pltpu.VMEM((8, 3 * BLK, 64), jnp.bfloat16),
        pltpu.VMEM((8, BLK, HALF), jnp.float32),
        pltpu.VMEM((9, 2, BANDS, HALF), jnp.float32),
    ]
    leaving, tiles, listed, counted, kept = pl.pallas_call(
        first_kernel,
        out_shape=[
            jax.ShapeDtypeStruct((units, BANDS, HALF), jnp.bfloat16),
            jax.ShapeDtypeStruct((KEPT + 8, BLK, BLK), jnp.bfloat16),
            jax.ShapeDtypeStruct((4 * peers + STEP2,), jnp.int32),
            jax.ShapeDtypeStruct((1,), jnp.int32),
            jax.ShapeDtypeStruct(geo.shape, jnp.float32),
        ],
        in_specs=[vmem] * 5,
        out_specs=[vmem, anywhere, smem, smem, anywhere],
        scratch_shapes=[
            pltpu.VMEM((peers, HALF), jnp.float32),
            pltpu.VMEM((8, peers), jnp.int32),
            pltpu.SMEM((8, peers), jnp.int32),
            pltpu.SemaphoreType.DMA(()),
        ]
        + scratch
        + [pltpu.VMEM((2, BLK, BLK), jnp.bfloat16)] * STEP
        + [pltpu.SemaphoreType.DMA((2, STEP))],
        compiler_params=pltpu.CompilerParams(vmem_limit_bytes=14 << 20),
        name="first_sweep",
    )(geo, flux.reshape(blocks, 2, BANDS, HALF), emission, material, reflect_table)
    (flux,) = gather_all([flux_units], LATER_PARTS, 1, [anywhere], [leaving])
    return pl.pallas_call(
        second_kernel,
        out_shape=jax.ShapeDtypeStruct((BANDS, patches), jnp.float32),
        in_specs=[smem, smem, anywhere] + [vmem] * 4 + [anywhere],
        out_specs=vmem,
        scratch_shapes=[
            pltpu.VMEM((blocks, 2, 8, HALF), jnp.float32),
            pltpu.SemaphoreType.DMA(()),
        ]
        + scratch
        + [
            pltpu.VMEM((1, BLK, BLK), jnp.bfloat16),
            pltpu.VMEM((DEPTH, STEP2, BLK, BLK), jnp.bfloat16),
            pltpu.SemaphoreType.DMA((DEPTH,)),
        ],
        compiler_params=pltpu.CompilerParams(vmem_limit_bytes=22 << 20),
        name="second_sweep",
    )(
        listed, counted, kept, flux.reshape(blocks, 2, BANDS, HALF), emission, material,
        reflect_table, tiles,
    )


def solution(mesh):
    placed = (
        P(None, AXES),
        P(None, AXES),
        P(None, AXES),
        P(AXES),
        P(AXES),
        P(),
        P(),
        P(AXES, None, None, None),
    )
    return jax.shard_map(
        per_device, mesh=mesh, in_specs=placed, out_specs=P(None, AXES), check_vma=False
    )
```

```python
import functools
import math

import jax
import jax.numpy as jnp
from jax import lax
from jax.experimental import pallas as pl
from jax.experimental.pallas import tpu as pltpu
from jax.sharding import PartitionSpec as P

MESH = pl.DeviceIdType.MESH
BANDS = 16
BLK = 256
HALF = 128
ITERS = 2
AXES = ("gx", "gy")
SIDE = 4
ORDERS = (("x", "y", "z"), ("y", "z", "x"), ("z", "x", "y"))
FIRST_PARTS = (((0, 11), (1, 5)), ((1, 6), (2, 10)))
LATER_PARTS = (((0, 6), (1, 5), (2, 5)),)
KEPT = 336
STEP = 8
STEP2 = 8
CHUNK = 64
DEPTH = 4
SKIP = 8 << 10
KAPPA = (math.pi - 1.0) / math.pi


def my_place():
    z = lax.axis_index("gx")
    inner = lax.axis_index("gy")
    place = {"z": z, "y": lax.div(inner, 2 * SIDE), "x": lax.rem(lax.div(inner, 2), SIDE)}
    return place, lax.rem(inner, 2)


def device_of(place, core):
    return (place["z"], (place["y"] * SIDE + place["x"]) * 2 + core)


def moved(place, axis, by):
    other = dict(place)
    other[axis] = lax.rem(place[axis] + (by + SIDE), SIDE)
    return other


def own_first(refs, srcs):
    geo_ref, flux_ref, *held, load_sem = srcs
    loads = [
        pltpu.make_async_copy(ref, to, load_sem.at[n]) for n, (ref, to) in enumerate(zip(refs, held))
    ]
    for load in loads:
        load.start()
    for load in loads:
        load.wait()
    position_ref, normal_ref, emission_ref, level_ref, area_ref, slot_ref = held
    for u in range(position_ref.shape[1] // HALF):
        lanes = slice(u * HALF, (u + 1) * HALF)
        level = level_ref[:, lanes]
        area = jnp.zeros(level.shape, jnp.float32)
        for m in range(area_ref.shape[1]):
            area = jnp.where(level == m, area_ref[0:1, m : m + 1], area)
        code = jnp.zeros(area.shape, jnp.float32)
        if u < 2:
            row, column = slot_ref[u, 0:1, :], slot_ref[u, 1:2, :]
            code = jnp.where(row >= 0, row * 8 + column, -1).astype(jnp.float32)
        geo_ref[u] = jnp.concatenate(
            [position_ref[:, lanes], area, normal_ref[:, lanes], code], axis=0
        )
        flux_ref[u] = (area * emission_ref[:, lanes]).astype(jnp.bfloat16)


def gather_kernel(parts, count, prologue, inputs, *refs):
    bufs, rest = refs[inputs : inputs + count], refs[inputs + count :]
    send_sem, recv_sem, local_sem = rest[:3]
    srcs = rest[3:] if prologue else refs[:count]
    here, core = my_place()
    other_core = device_of(here, 1 - core)
    barrier = pltpu.get_barrier_semaphore()
    peers = [device_of(moved(here, axis, by), core) for axis in "zyx" for by in (1, -1, 2)]
    peers.append(other_core)
    for peer in peers:
        pl.semaphore_signal(barrier, inc=1, device_id=peer, device_id_type=MESH)
    if prologue:
        prologue(refs[:inputs], srcs)
    own_copies = []
    for b in range(count):
        place = bufs[b].at[here["z"], here["y"], here["x"], core]
        own_copies.append(pltpu.make_async_copy(srcs[b], place, local_sem.at[b]))
        own_copies[-1].start()
    pl.semaphore_wait(barrier, len(peers))
    started = []
    shared = []

    def send(src, dst, to):
        n = len(started)
        copy = pltpu.make_async_remote_copy(
            src_ref=src,
            dst_ref=dst,
            send_sem=send_sem.at[n],
            recv_sem=recv_sem.at[n],
            device_id=to,
            device_id_type=MESH,
        )
        copy.start()
        started.append(copy)
        return copy

    def view(b, index, first, size):
        return bufs[b].at[index["z"], index["y"], index["x"], core, pl.ds(first, size)]

    def share(b, index, first, size):
        piece = view(b, index, first, size)
        shared.append(send(piece, piece, other_core))

    work = []
    for b in range(count):
        first = 0
        for k, size in parts[b]:
            work.append((b, k, first, size))
            first += size

    for copy in own_copies:
        copy.wait()

    def at(k, line, plane, far):
        index = {}
        for axis, by in zip(ORDERS[k], (line, plane, far)):
            index[axis] = pl.ds(0, SIDE) if by is None else moved(here, axis, by)[axis]
        return index

    def to(k, stage, by):
        return device_of(moved(here, ORDERS[k][stage], by), core)

    def pass_on(item, stage, by, index):
        b, k, first, size = item
        piece = view(b, index, first, size)
        return send(piece, piece, to(k, stage, by))

    def half(k, index, which):
        index = dict(index)
        index[ORDERS[k][0]] = pl.ds(2 * which, 2)
        return index

    line, plane, ahead, far, again = {}, {}, {}, {}, {}
    for item in work:
        b, k, first, size = item
        src, dst = srcs[b].at[pl.ds(first, size)], view(b, here, first, size)
        line[item] = [send(src, dst, to(k, 0, by)) for by in (1, -1, 2)]
    for item in work:
        b, k, first, size = item
        for copy in line[item]:
            copy.wait_recv()
        mine = at(k, None, 0, 0)
        plane[item] = {by: pass_on(item, 1, by, mine) for by in (1, -1)}
        for by in (1, -1):
            far[item, 0, by] = pass_on(item, 2, by, mine)
        share(b, mine, first, size)
    for item in work:
        b, k, first, size = item
        plane[item][1].wait_recv()
        up = pass_on(item, 1, 1, half(k, at(k, None, -1, 0), 0))
        plane[item][-1].wait_recv()
        down = pass_on(item, 1, -1, half(k, at(k, None, 1, 0), 1))
        ahead[item] = [up, down]
        for row in (-1, 1):
            index = at(k, None, row, 0)
            for by in (1, -1):
                far[item, row, by] = pass_on(item, 2, by, index)
            share(b, index, first, size)

    def forward(item, row):
        k = item[1]
        far[item, row, 1].wait_recv()
        up = pass_on(item, 2, 1, half(k, at(k, None, row, -1), 0))
        far[item, row, -1].wait_recv()
        down = pass_on(item, 2, -1, half(k, at(k, None, row, 1), 1))
        again[item, row] = [up, down]

    def share_far(item, row):
        b, k, first, size = item
        share(b, at(k, None, row, -1), first, size)
        share(b, at(k, None, row, 1), first, size)

    for item in work:
        forward(item, 0)
        share_far(item, 0)
    for item in work:
        b, k, first, size = item
        for copy in ahead[item]:
            copy.wait_recv()
        index = at(k, None, 2, 0)
        for by in (1, -1):
            far[item, 2, by] = pass_on(item, 2, by, index)
        share(b, index, first, size)
    for row in (-1, 1, 2):
        for item in work:
            forward(item, row)
            share_far(item, row)
    for row in (0, -1, 1, 2):
        for item in work:
            b, k, first, size = item
            for copy in again[item, row]:
                copy.wait_recv()
            if row == 1:
                pass
            share(b, at(k, None, row, 2), first, size)
    for copy in shared:
        copy.wait_recv()
    for copy in started:
        copy.wait_send()


def gather_all(shapes, parts, collective_id, specs, inputs, prologue=None):
    count = len(shapes)
    copies = 39 * sum(len(p) for p in parts)
    own = []
    if prologue:
        own = [pltpu.VMEM(a.shape, a.dtype) for a in list(shapes) + list(inputs)]
        own.append(pltpu.SemaphoreType.DMA((len(inputs),)))
    return pl.pallas_call(
        functools.partial(gather_kernel, parts, count, prologue, len(inputs)),
        out_shape=[
            jax.ShapeDtypeStruct((SIDE, SIDE, SIDE, 2) + a.shape, a.dtype) for a in shapes
        ],
        in_specs=specs,
        out_specs=[pl.BlockSpec(memory_space=pl.ANY)] * count,
        scratch_shapes=[
            pltpu.SemaphoreType.DMA((copies,)),
            pltpu.SemaphoreType.DMA((copies,)),
            pltpu.SemaphoreType.DMA((count,)),
        ]
        + own,
        compiler_params=pltpu.CompilerParams(
            collective_id=collective_id, has_side_effects=True, vmem_limit_bytes=2 << 20
        ),
        name="gather_all",
    )(*inputs)


def my_block():
    return (lax.axis_index("gx") * lax.axis_size("gy") + lax.axis_index("gy")) * 8


def reflect_of(table_ref, material_ref, lanes):
    material = material_ref[:, lanes]
    kinds = table_ref.shape[0]
    hot = lax.broadcasted_iota(jnp.int32, (kinds, HALF), 0) == material
    return lax.dot_general(
        table_ref[...],
        jnp.where(hot, 1.0, 0.0),
        (((0,), (0,)), ((), ())),
        precision=lax.Precision.HIGHEST,
        preferred_element_type=jnp.float32,
    )


def split3(x):
    a = x.astype(jnp.bfloat16).astype(jnp.float32)
    rest = x - a
    b = rest.astype(jnp.bfloat16).astype(jnp.float32)
    return a, b, rest - b


def block_of(ref, b):
    return jnp.concatenate([ref[b, 0], ref[b, 1]], axis=1)


def centred(rows, centre):
    moved_rows = rows - centre
    squares = moved_rows * moved_rows
    cross = moved_rows * pltpu.roll(moved_rows, 4, 0)
    reach = (squares[0:1] + squares[1:2] + squares[2:3]) + 0.5 * rows[3:4]
    plane = -(cross[0:1] + cross[1:2] + cross[2:3])
    return moved_rows, reach, plane


def source_rows(rows, centre):
    at = lax.broadcasted_iota(jnp.int32, rows.shape, 0)
    base, reach, plane = centred(rows, centre)
    base = jnp.where(at == 3, reach, jnp.where(at == 7, plane, base))
    a, b, c = split3(base)
    one = jnp.where(at < 3, 1.0, 0.0)
    stacked = jnp.concatenate([a, a, a, b, b, c, one, jnp.zeros_like(one)], axis=0)
    return stacked.astype(jnp.bfloat16), (KAPPA * 0.5) * rows[3:4]


def target_columns(rows, centre):
    at = lax.broadcasted_iota(jnp.int32, rows.shape, 0)
    base, reach, plane = centred(rows, centre)
    zero = jnp.zeros_like(base)
    swapped = pltpu.roll(base, 4, 0)
    facing = jnp.where(at < 3, swapped, 0.0) * (1.0 / math.pi)
    seen = jnp.where((at >= 4) & (at < 7), swapped, jnp.where(at == 7, 1.0, 0.0))
    spread = jnp.where(at < 3, -2.0 * base, jnp.where(at == 3, 1.0, 0.0))
    columns = []
    for factor, constant in ((facing, plane * (1.0 / math.pi)), (seen, None), (spread, reach)):
        a, b, c = split3(factor)
        last = zero
        if constant is not None:
            d, e, f = split3(constant)
            last = jnp.where(at == 0, d, jnp.where(at == 1, e, jnp.where(at == 2, f, 0.0)))
        stacked = jnp.concatenate([a, b, c, a, b, a, last, zero], axis=0)
        columns.append(jnp.transpose(stacked).astype(jnp.bfloat16))
    return columns, (KAPPA * 0.5) * rows[3:4]


def prepare_targets(geo_ref, centre_ref, column_ref, offset_ref):
    for t in range(8):
        rows = block_of(geo_ref, my_block() + t)
        at = lax.broadcasted_iota(jnp.int32, rows.shape, 0)
        centre = jnp.where(at < 3, jnp.broadcast_to(rows[:, 0:1], rows.shape), 0.0)
        centre_ref[t] = centre
        columns, offset = target_columns(rows, centre)
        for r in range(0, BLK, CHUNK):
            column_ref[t, 3 * r : 3 * (r + CHUNK)] = jnp.concatenate(
                [c[r : r + CHUNK] for c in columns], axis=0
            )
        offset_ref[t] = jnp.transpose(jnp.broadcast_to(offset, (HALF, BLK)))


def build_tile(t, b, geo_ref, centre_ref, column_ref, offset_ref, tile_ref, slot):
    source, source_offset = source_rows(block_of(geo_ref, b), centre_ref[t])
    for r in range(0, BLK, CHUNK):
        terms = jnp.dot(
            column_ref[t, 3 * r : 3 * (r + CHUNK), :], source, preferred_element_type=jnp.float32
        )
        facing, seen, spread = terms[:CHUNK], terms[CHUNK : 2 * CHUNK], terms[2 * CHUNK :]
        offset = offset_ref[t, r : r + CHUNK, :]
        offset = jnp.concatenate([offset, offset], axis=1)
        over = jnp.maximum(facing, 0.0) * jnp.maximum(seen, 0.0)
        under = spread * ((spread - offset) - source_offset)
        tile_ref[slot, r : r + CHUNK, :] = (over / under).astype(jnp.bfloat16)


def add_product(t, flux, tile, sum_ref):
    term = lax.dot_general(
        flux, tile, (((1,), (1,)), ((), ())), preferred_element_type=jnp.float32
    )
    sum_ref[t, 0] += term[:, :HALF]
    sum_ref[t, 1] += term[:, HALF:]


def decode(code):
    t = lax.shift_right_logical(code, 10)
    return t, jnp.minimum(t, 7), lax.bitwise_and(code, 1023)


def first_kernel(
    geo_ref, flux_ref, emission_all, material_all, table_all,
    leaving_ref, tiles_ref, list_ref, count_ref, kept_ref,
    emission_ref, material_ref, table_ref, load_sem, code_ref, entry_ref, slot_ref, slot_sem, centre_ref, column_ref, offset_ref, sum_ref, *rest,
):
    bufs, sem = rest[:STEP], rest[STEP]
    loads = [
        pltpu.make_async_copy(emission_all, emission_ref, load_sem.at[0]),
        pltpu.make_async_copy(material_all, material_ref, load_sem.at[1]),
        pltpu.make_async_copy(table_all, table_ref, load_sem.at[2]),
    ]
    for load in loads:
        load.start()
    first = my_block()
    peers = geo_ref.shape[0] // 8
    peer = lax.broadcasted_iota(jnp.int32, (1, peers), 1)
    at_me = lax.broadcasted_iota(jnp.int32, (8, HALF), 1) == lax.div(first, 8)
    pick = jnp.where(at_me, 1.0, 0.0).astype(jnp.bfloat16)
    entry_ref[...] = jnp.full_like(entry_ref, -1)
    for c in range(2):
        for p in range(peers):
            code_ref[p : p + 1, :] = geo_ref[p * 8, c, 7:8, :]
        served = lax.dot_general(
            pick,
            code_ref[...].astype(jnp.bfloat16),
            (((1,), (1,)), ((), ())),
            preferred_element_type=jnp.float32,
        )[0:1].astype(jnp.int32)
        owned = geo_ref[first, c, 7:8, :].astype(jnp.int32)
        for row, code, own in ((c, owned, True), (2 + c, served, False)):
            high, low = lax.shift_right_arithmetic(code, 3), lax.bitwise_and(code, 7)
            target, source = (high, low) if own else (low, high)
            entry_ref[row : row + 1, :] = jnp.where(
                code >= 0, target * 1024 + peer * 8 + source, -1
            )
    slot_copy = pltpu.make_async_copy(entry_ref, slot_ref, slot_sem)
    slot_copy.start()
    prepare_targets(geo_ref, centre_ref, column_ref, offset_ref)
    sum_ref[...] = jnp.zeros_like(sum_ref)
    slot_copy.wait()
    bufs[-1][1] = jnp.zeros_like(bufs[-1][1])

    def compact(e, n):
        for k in range(8):
            code = slot_ref[lax.div(e, HALF // 8), lax.rem(e, HALF // 8) * 8 + k]
            list_ref[n] = code
            n = n + jnp.where(code >= 0, 1, 0)
        return n

    n = lax.fori_loop(0, 4 * HALF // 8, compact, 0)
    for k in range(STEP2):
        list_ref[n + k] = SKIP
    count_ref[0] = n

    @pl.when(n > KEPT)
    def _():
        keep = pltpu.make_async_copy(geo_ref, kept_ref, slot_sem)
        keep.start()
        keep.wait()

    rounds = pl.cdiv(n, STEP)

    def out_copy(i, k):
        side = lax.rem(i, 2)
        to = jnp.minimum(i * STEP + k, KEPT)
        return pltpu.make_async_copy(bufs[k].at[side], tiles_ref.at[to], sem.at[side, k])

    def add_tile(code, k, side):
        t, held, b = decode(code)
        add_product(t, block_of(flux_ref, b), bufs[k][side], sum_ref)

    def step(i, carry):
        @pl.when(i >= 2)
        def _():
            for k in range(STEP):
                out_copy(i - 2, k).wait()

        side = lax.rem(i, 2)
        before = jnp.where(i > 0, list_ref[jnp.maximum(i * STEP - 1, 0)], SKIP)
        for k in range(STEP):
            code = list_ref[i * STEP + k]
            t, held, b = decode(code)
            build_tile(held, b, geo_ref, centre_ref, column_ref, offset_ref, bufs[k], side)
            if k == 0:
                add_tile(before, STEP - 1, 1 - side)
            else:
                add_tile(before, k - 1, side)
            before = code
        for k in range(STEP):
            out_copy(i, k).start()
        return carry

    lax.fori_loop(0, rounds, step, 0)
    last = jnp.where(rounds > 0, list_ref[jnp.maximum(rounds * STEP - 1, 0)], SKIP)
    add_tile(last, STEP - 1, lax.rem(rounds + 1, 2))
    for back in (2, 1):

        @pl.when(rounds >= back)
        def _():
            for k in range(STEP):
                out_copy(rounds - back, k).wait()

    for load in loads:
        load.wait()
    for u in range(16):
        lanes = slice(u * HALF, (u + 1) * HALF)
        reflect = reflect_of(table_ref, material_ref, lanes)
        radiosity = emission_ref[:, lanes] + reflect * sum_ref[u // 2, u % 2]
        area = geo_ref[first + u // 2, u % 2, 3:4, :]
        leaving_ref[u] = (area * radiosity).astype(jnp.bfloat16)


def second_kernel(
    list_ref, count_ref, geo_all, flux_ref, emission_ref, material_ref, table_ref, tiles_ref,
    out_ref,
    geo_ref, load_sem, centre_ref, column_ref, offset_ref, sum_ref, spare_ref, buf_ref, sem,
):
    n = count_ref[0]
    rounds = pl.cdiv(jnp.minimum(n, KEPT), STEP2)

    def in_copy(i):
        side = lax.rem(i, DEPTH)
        return pltpu.make_async_copy(
            tiles_ref.at[pl.ds(i * STEP2, STEP2)], buf_ref.at[side], sem.at[side]
        )

    for i in range(DEPTH - 1):

        @pl.when(i < rounds)
        def _():
            in_copy(i).start()

    sum_ref[...] = jnp.zeros_like(sum_ref)

    def step(i, carry):
        @pl.when(i + DEPTH - 1 < rounds)
        def _():
            in_copy(i + DEPTH - 1).start()

        in_copy(i).wait()
        side = lax.rem(i, DEPTH)
        for k in range(STEP2):
            t, held, b = decode(list_ref[i * STEP2 + k])
            add_product(t, block_of(flux_ref, b), buf_ref[side, k], sum_ref)
        return carry

    lax.fori_loop(0, rounds, step, 0)

    @pl.when(n > KEPT)
    def _():
        again_load = pltpu.make_async_copy(geo_all, geo_ref, load_sem)
        again_load.start()
        again_load.wait()
        prepare_targets(geo_ref, centre_ref, column_ref, offset_ref)

        def again(e, carry):
            t, held, b = decode(list_ref[e])
            build_tile(held, b, geo_ref, centre_ref, column_ref, offset_ref, spare_ref, 0)
            add_product(t, block_of(flux_ref, b), spare_ref[0], sum_ref)
            return carry

        lax.fori_loop(KEPT, n, again, 0)

    for u in range(16):
        lanes = slice(u * HALF, (u + 1) * HALF)
        reflect = reflect_of(table_ref, material_ref, lanes)
        out_ref[:, lanes] = emission_ref[:, lanes] + reflect * sum_ref[u // 2, u % 2]


def per_device(
    positions, normals, emission, material, area_level, reflect_table, area_table, pair_slots
):
    patches = positions.shape[1]
    units = patches // HALF
    peers = pair_slots.shape[1]
    blocks = peers * 8
    vmem = pl.BlockSpec(memory_space=pltpu.VMEM)
    smem = pl.BlockSpec(memory_space=pltpu.SMEM)
    anywhere = pl.BlockSpec(memory_space=pl.ANY)
    resident = pl.BlockSpec(memory_space=pltpu.HBM)
    material, level = material.reshape(1, patches), area_level.reshape(1, patches)
    slots = jnp.transpose(pair_slots[0], (1, 2, 0))
    pin = lambda x: pltpu.with_memory_space_constraint(x, pltpu.HBM)
    geo_units = jax.ShapeDtypeStruct((units, 8, HALF), jnp.float32)
    flux_units = jax.ShapeDtypeStruct((units, BANDS, HALF), jnp.bfloat16)
    geo, flux = gather_all(
        [geo_units, flux_units],
        FIRST_PARTS,
        0,
        [resident] * 6,
        [pin(x) for x in (positions, normals, emission, level, area_table.reshape(1, -1), slots)],
        own_first,
    )
    geo = geo.reshape(blocks, 2, 8, HALF)

    scratch = [
        pltpu.VMEM((8, 8, BLK), jnp.float32),
        pltpu.VMEM((8, 3 * BLK, 64), jnp.bfloat16),
        pltpu.VMEM((8, BLK, HALF), jnp.float32),
        pltpu.VMEM((9, 2, BANDS, HALF), jnp.float32),
    ]
    leaving, tiles, listed, counted, kept = pl.pallas_call(
        first_kernel,
        out_shape=[
            jax.ShapeDtypeStruct((units, BANDS, HALF), jnp.bfloat16),
            jax.ShapeDtypeStruct((KEPT + 8, BLK, BLK), jnp.bfloat16),
            jax.ShapeDtypeStruct((4 * peers + STEP2,), jnp.int32),
            jax.ShapeDtypeStruct((1,), jnp.int32),
            jax.ShapeDtypeStruct(geo.shape, jnp.float32),
        ],
        in_specs=[vmem] * 2 + [resident] * 3,
        out_specs=[vmem, anywhere, smem, smem, anywhere],
        scratch_shapes=[
            pltpu.VMEM(emission.shape, jnp.float32),
            pltpu.VMEM(material.shape, jnp.int32),
            pltpu.VMEM(reflect_table.shape, jnp.float32),
            pltpu.SemaphoreType.DMA((3,)),
            pltpu.VMEM((peers, HALF), jnp.float32),
            pltpu.VMEM((8, peers), jnp.int32),
            pltpu.SMEM((8, peers), jnp.int32),
            pltpu.SemaphoreType.DMA(()),
        ]
        + scratch
        + [pltpu.VMEM((2, BLK, BLK), jnp.bfloat16)] * STEP
        + [pltpu.SemaphoreType.DMA((2, STEP))],
        compiler_params=pltpu.CompilerParams(vmem_limit_bytes=14 << 20),
        name="first_sweep",
    )(geo, flux.reshape(blocks, 2, BANDS, HALF), pin(emission), pin(material), pin(reflect_table))
    (flux,) = gather_all([flux_units], LATER_PARTS, 1, [anywhere], [leaving])
    return pl.pallas_call(
        second_kernel,
        out_shape=jax.ShapeDtypeStruct((BANDS, patches), jnp.float32),
        in_specs=[smem, smem, anywhere] + [vmem] * 4 + [anywhere],
        out_specs=vmem,
        scratch_shapes=[
            pltpu.VMEM((blocks, 2, 8, HALF), jnp.float32),
            pltpu.SemaphoreType.DMA(()),
        ]
        + scratch
        + [
            pltpu.VMEM((1, BLK, BLK), jnp.bfloat16),
            pltpu.VMEM((DEPTH, STEP2, BLK, BLK), jnp.bfloat16),
            pltpu.SemaphoreType.DMA((DEPTH,)),
        ],
        compiler_params=pltpu.CompilerParams(vmem_limit_bytes=22 << 20),
        name="second_sweep",
    )(
        listed, counted, kept, flux.reshape(blocks, 2, BANDS, HALF), emission, material,
        reflect_table, tiles,
    )


def solution(mesh):
    placed = (
        P(None, AXES),
        P(None, AXES),
        P(None, AXES),
        P(AXES),
        P(AXES),
        P(),
        P(),
        P(AXES, None, None, None),
    )
    return jax.shard_map(
        per_device, mesh=mesh, in_specs=placed, out_specs=P(None, AXES), check_vma=False
    )
```

```python
import functools
import math

import jax
import jax.numpy as jnp
from jax import lax
from jax.experimental import pallas as pl
from jax.experimental.pallas import tpu as pltpu
from jax.sharding import PartitionSpec as P

MESH = pl.DeviceIdType.MESH
BANDS = 16
BLK = 256
HALF = 128
ITERS = 2
AXES = ("gx", "gy")
SIDE = 4
ORDERS = (("x", "y", "z"), ("y", "z", "x"), ("z", "x", "y"))
FIRST_PARTS = (((0, 11), (1, 5)), ((1, 6), (2, 10)))
LATER_PARTS = (((0, 6), (1, 5), (2, 5)),)
KEPT = 336
STEP = 16
STEP2 = 16
CHUNK = 64
DEPTH = 4
SKIP = 8 << 10
KAPPA = (math.pi - 1.0) / math.pi


def my_place():
    z = lax.axis_index("gx")
    inner = lax.axis_index("gy")
    place = {"z": z, "y": lax.div(inner, 2 * SIDE), "x": lax.rem(lax.div(inner, 2), SIDE)}
    return place, lax.rem(inner, 2)


def device_of(place, core):
    return (place["z"], (place["y"] * SIDE + place["x"]) * 2 + core)


def moved(place, axis, by):
    other = dict(place)
    other[axis] = lax.rem(place[axis] + (by + SIDE), SIDE)
    return other


def own_first(refs, srcs):
    geo_ref, flux_ref, *held, load_sem = srcs
    loads = [
        pltpu.make_async_copy(ref, to, load_sem.at[n]) for n, (ref, to) in enumerate(zip(refs, held))
    ]
    for load in loads:
        load.start()
    for load in loads:
        load.wait()
    position_ref, normal_ref, emission_ref, level_ref, area_ref, slot_ref = held
    for u in range(position_ref.shape[1] // HALF):
        lanes = slice(u * HALF, (u + 1) * HALF)
        level = level_ref[:, lanes]
        area = jnp.zeros(level.shape, jnp.float32)
        for m in range(area_ref.shape[1]):
            area = jnp.where(level == m, area_ref[0:1, m : m + 1], area)
        code = jnp.zeros(area.shape, jnp.float32)
        if u < 2:
            row, column = slot_ref[u, 0:1, :], slot_ref[u, 1:2, :]
            code = jnp.where(row >= 0, row * 8 + column, -1).astype(jnp.float32)
        geo_ref[u] = jnp.concatenate(
            [position_ref[:, lanes], area, normal_ref[:, lanes], code], axis=0
        )
        flux_ref[u] = (area * emission_ref[:, lanes]).astype(jnp.bfloat16)


def gather_kernel(parts, count, prologue, inputs, *refs):
    bufs, rest = refs[inputs : inputs + count], refs[inputs + count :]
    send_sem, recv_sem, local_sem = rest[:3]
    srcs = rest[3:] if prologue else refs[:count]
    here, core = my_place()
    other_core = device_of(here, 1 - core)
    barrier = pltpu.get_barrier_semaphore()
    peers = [device_of(moved(here, axis, by), core) for axis in "zyx" for by in (1, -1, 2)]
    peers.append(other_core)
    for peer in peers:
        pl.semaphore_signal(barrier, inc=1, device_id=peer, device_id_type=MESH)
    if prologue:
        prologue(refs[:inputs], srcs)
    own_copies = []
    for b in range(count):
        place = bufs[b].at[here["z"], here["y"], here["x"], core]
        own_copies.append(pltpu.make_async_copy(srcs[b], place, local_sem.at[b]))
        own_copies[-1].start()
    pl.semaphore_wait(barrier, len(peers))
    started = []
    shared = []

    def send(src, dst, to):
        n = len(started)
        copy = pltpu.make_async_remote_copy(
            src_ref=src,
            dst_ref=dst,
            send_sem=send_sem.at[n],
            recv_sem=recv_sem.at[n],
            device_id=to,
            device_id_type=MESH,
        )
        copy.start()
        started.append(copy)
        return copy

    def view(b, index, first, size):
        return bufs[b].at[index["z"], index["y"], index["x"], core, pl.ds(first, size)]

    def share(b, index, first, size):
        piece = view(b, index, first, size)
        shared.append(send(piece, piece, other_core))

    work = []
    for b in range(count):
        first = 0
        for k, size in parts[b]:
            work.append((b, k, first, size))
            first += size

    for copy in own_copies:
        copy.wait()

    def at(k, line, plane, far):
        index = {}
        for axis, by in zip(ORDERS[k], (line, plane, far)):
            index[axis] = pl.ds(0, SIDE) if by is None else moved(here, axis, by)[axis]
        return index

    def to(k, stage, by):
        return device_of(moved(here, ORDERS[k][stage], by), core)

    def pass_on(item, stage, by, index):
        b, k, first, size = item
        piece = view(b, index, first, size)
        return send(piece, piece, to(k, stage, by))

    def half(k, index, which):
        index = dict(index)
        index[ORDERS[k][0]] = pl.ds(2 * which, 2)
        return index

    line, plane, ahead, far, again = {}, {}, {}, {}, {}
    for item in work:
        b, k, first, size = item
        src, dst = srcs[b].at[pl.ds(first, size)], view(b, here, first, size)
        line[item] = [send(src, dst, to(k, 0, by)) for by in (1, -1, 2)]
    for item in work:
        b, k, first, size = item
        for copy in line[item]:
            copy.wait_recv()
        mine = at(k, None, 0, 0)
        plane[item] = {by: pass_on(item, 1, by, mine) for by in (1, -1)}
        for by in (1, -1):
            far[item, 0, by] = pass_on(item, 2, by, mine)
        share(b, mine, first, size)
    for item in work:
        b, k, first, size = item
        plane[item][1].wait_recv()
        up = pass_on(item, 1, 1, half(k, at(k, None, -1, 0), 0))
        plane[item][-1].wait_recv()
        down = pass_on(item, 1, -1, half(k, at(k, None, 1, 0), 1))
        ahead[item] = [up, down]
        for row in (-1, 1):
            index = at(k, None, row, 0)
            for by in (1, -1):
                far[item, row, by] = pass_on(item, 2, by, index)
            share(b, index, first, size)

    def forward(item, row):
        k = item[1]
        far[item, row, 1].wait_recv()
        up = pass_on(item, 2, 1, half(k, at(k, None, row, -1), 0))
        far[item, row, -1].wait_recv()
        down = pass_on(item, 2, -1, half(k, at(k, None, row, 1), 1))
        again[item, row] = [up, down]

    def share_far(item, row):
        b, k, first, size = item
        share(b, at(k, None, row, -1), first, size)
        share(b, at(k, None, row, 1), first, size)

    for item in work:
        forward(item, 0)
        share_far(item, 0)
    for item in work:
        b, k, first, size = item
        for copy in ahead[item]:
            copy.wait_recv()
        index = at(k, None, 2, 0)
        for by in (1, -1):
            far[item, 2, by] = pass_on(item, 2, by, index)
        share(b, index, first, size)
    for row in (-1, 1, 2):
        for item in work:
            forward(item, row)
            share_far(item, row)
    for row in (0, -1, 1, 2):
        for item in work:
            b, k, first, size = item
            for copy in again[item, row]:
                copy.wait_recv()
            share(b, at(k, None, row, 2), first, size)
    for copy in shared:
        copy.wait_recv()
    for copy in started:
        copy.wait_send()


def gather_all(shapes, parts, collective_id, specs, inputs, prologue=None):
    count = len(shapes)
    copies = 39 * sum(len(p) for p in parts)
    own = []
    if prologue:
        own = [pltpu.VMEM(a.shape, a.dtype) for a in list(shapes) + list(inputs)]
        own.append(pltpu.SemaphoreType.DMA((len(inputs),)))
    return pl.pallas_call(
        functools.partial(gather_kernel, parts, count, prologue, len(inputs)),
        out_shape=[
            jax.ShapeDtypeStruct((SIDE, SIDE, SIDE, 2) + a.shape, a.dtype) for a in shapes
        ],
        in_specs=specs,
        out_specs=[pl.BlockSpec(memory_space=pl.ANY)] * count,
        scratch_shapes=[
            pltpu.SemaphoreType.DMA((copies,)),
            pltpu.SemaphoreType.DMA((copies,)),
            pltpu.SemaphoreType.DMA((count,)),
        ]
        + own,
        compiler_params=pltpu.CompilerParams(
            collective_id=collective_id, has_side_effects=True, vmem_limit_bytes=2 << 20
        ),
        name="gather_all",
    )(*inputs)


def my_block():
    return (lax.axis_index("gx") * lax.axis_size("gy") + lax.axis_index("gy")) * 8


def reflect_of(table_ref, material_ref, lanes):
    material = material_ref[:, lanes]
    kinds = table_ref.shape[0]
    hot = lax.broadcasted_iota(jnp.int32, (kinds, HALF), 0) == material
    return lax.dot_general(
        table_ref[...],
        jnp.where(hot, 1.0, 0.0),
        (((0,), (0,)), ((), ())),
        precision=lax.Precision.HIGHEST,
        preferred_element_type=jnp.float32,
    )


def split3(x):
    a = x.astype(jnp.bfloat16).astype(jnp.float32)
    rest = x - a
    b = rest.astype(jnp.bfloat16).astype(jnp.float32)
    return a, b, rest - b


def block_of(ref, b):
    return jnp.concatenate([ref[b, 0], ref[b, 1]], axis=1)


def centred(rows, centre):
    moved_rows = rows - centre
    squares = moved_rows * moved_rows
    cross = moved_rows * pltpu.roll(moved_rows, 4, 0)
    reach = (squares[0:1] + squares[1:2] + squares[2:3]) + 0.5 * rows[3:4]
    plane = -(cross[0:1] + cross[1:2] + cross[2:3])
    return moved_rows, reach, plane


def source_rows(rows, centre):
    at = lax.broadcasted_iota(jnp.int32, rows.shape, 0)
    base, reach, plane = centred(rows, centre)
    base = jnp.where(at == 3, reach, jnp.where(at == 7, plane, base))
    a, b, c = split3(base)
    one = jnp.where(at < 3, 1.0, 0.0)
    stacked = jnp.concatenate([a, a, a, b, b, c, one, jnp.zeros_like(one)], axis=0)
    return stacked.astype(jnp.bfloat16), (KAPPA * 0.5) * rows[3:4]


def target_columns(rows, centre):
    at = lax.broadcasted_iota(jnp.int32, rows.shape, 0)
    base, reach, plane = centred(rows, centre)
    zero = jnp.zeros_like(base)
    swapped = pltpu.roll(base, 4, 0)
    facing = jnp.where(at < 3, swapped, 0.0) * (1.0 / math.pi)
    seen = jnp.where((at >= 4) & (at < 7), swapped, jnp.where(at == 7, 1.0, 0.0))
    spread = jnp.where(at < 3, -2.0 * base, jnp.where(at == 3, 1.0, 0.0))
    columns = []
    for factor, constant in ((facing, plane * (1.0 / math.pi)), (seen, None), (spread, reach)):
        a, b, c = split3(factor)
        last = zero
        if constant is not None:
            d, e, f = split3(constant)
            last = jnp.where(at == 0, d, jnp.where(at == 1, e, jnp.where(at == 2, f, 0.0)))
        stacked = jnp.concatenate([a, b, c, a, b, a, last, zero], axis=0)
        columns.append(jnp.transpose(stacked).astype(jnp.bfloat16))
    return columns, (KAPPA * 0.5) * rows[3:4]


def prepare_targets(geo_ref, centre_ref, column_ref, offset_ref):
    for t in range(8):
        rows = block_of(geo_ref, my_block() + t)
        at = lax.broadcasted_iota(jnp.int32, rows.shape, 0)
        centre = jnp.where(at < 3, jnp.broadcast_to(rows[:, 0:1], rows.shape), 0.0)
        centre_ref[t] = centre
        columns, offset = target_columns(rows, centre)
        for r in range(0, BLK, CHUNK):
            column_ref[t, 3 * r : 3 * (r + CHUNK)] = jnp.concatenate(
                [c[r : r + CHUNK] for c in columns], axis=0
            )
        offset_ref[t] = jnp.transpose(jnp.broadcast_to(offset, (HALF, BLK)))


def build_tile(t, b, geo_ref, centre_ref, column_ref, offset_ref, tile_ref, slot):
    source, source_offset = source_rows(block_of(geo_ref, b), centre_ref[t])
    for r in range(0, BLK, CHUNK):
        terms = jnp.dot(
            column_ref[t, 3 * r : 3 * (r + CHUNK), :], source, preferred_element_type=jnp.float32
        )
        facing, seen, spread = terms[:CHUNK], terms[CHUNK : 2 * CHUNK], terms[2 * CHUNK :]
        offset = offset_ref[t, r : r + CHUNK, :]
        offset = jnp.concatenate([offset, offset], axis=1)
        over = jnp.maximum(facing, 0.0) * jnp.maximum(seen, 0.0)
        under = spread * ((spread - offset) - source_offset)
        tile_ref[slot, r : r + CHUNK, :] = (over / under).astype(jnp.bfloat16)


def add_product(t, flux, tile, sum_ref):
    term = lax.dot_general(
        flux, tile, (((1,), (1,)), ((), ())), preferred_element_type=jnp.float32
    )
    sum_ref[t, 0] += term[:, :HALF]
    sum_ref[t, 1] += term[:, HALF:]


def decode(code):
    t = lax.shift_right_logical(code, 10)
    return t, jnp.minimum(t, 7), lax.bitwise_and(code, 1023)


def first_kernel(
    geo_ref, flux_ref, emission_all, material_all, table_all,
    leaving_ref, tiles_ref, list_ref, count_ref, kept_ref,
    emission_ref, material_ref, table_ref, load_sem, code_ref, entry_ref, slot_ref, slot_sem, centre_ref, column_ref, offset_ref, sum_ref, *rest,
):
    bufs, sem = rest[:STEP], rest[STEP]
    loads = [
        pltpu.make_async_copy(emission_all, emission_ref, load_sem.at[0]),
        pltpu.make_async_copy(material_all, material_ref, load_sem.at[1]),
        pltpu.make_async_copy(table_all, table_ref, load_sem.at[2]),
    ]
    for load in loads:
        load.start()
    first = my_block()
    peers = geo_ref.shape[0] // 8
    peer = lax.broadcasted_iota(jnp.int32, (1, peers), 1)
    at_me = lax.broadcasted_iota(jnp.int32, (8, HALF), 1) == lax.div(first, 8)
    pick = jnp.where(at_me, 1.0, 0.0).astype(jnp.bfloat16)
    entry_ref[...] = jnp.full_like(entry_ref, -1)
    for c in range(2):
        for p in range(peers):
            code_ref[p : p + 1, :] = geo_ref[p * 8, c, 7:8, :]
        served = lax.dot_general(
            pick,
            code_ref[...].astype(jnp.bfloat16),
            (((1,), (1,)), ((), ())),
            preferred_element_type=jnp.float32,
        )[0:1].astype(jnp.int32)
        owned = geo_ref[first, c, 7:8, :].astype(jnp.int32)
        for row, code, own in ((c, owned, True), (2 + c, served, False)):
            high, low = lax.shift_right_arithmetic(code, 3), lax.bitwise_and(code, 7)
            target, source = (high, low) if own else (low, high)
            entry_ref[row : row + 1, :] = jnp.where(
                code >= 0, target * 1024 + peer * 8 + source, -1
            )
    slot_copy = pltpu.make_async_copy(entry_ref, slot_ref, slot_sem)
    slot_copy.start()
    prepare_targets(geo_ref, centre_ref, column_ref, offset_ref)
    sum_ref[...] = jnp.zeros_like(sum_ref)
    slot_copy.wait()
    bufs[-1][1] = jnp.zeros_like(bufs[-1][1])

    def compact(e, n):
        for k in range(8):
            code = slot_ref[lax.div(e, HALF // 8), lax.rem(e, HALF // 8) * 8 + k]
            list_ref[n] = code
            n = n + jnp.where(code >= 0, 1, 0)
        return n

    n = lax.fori_loop(0, 4 * HALF // 8, compact, 0)
    for k in range(STEP2):
        list_ref[n + k] = SKIP
    count_ref[0] = n

    @pl.when(n > KEPT)
    def _():
        keep = pltpu.make_async_copy(geo_ref, kept_ref, slot_sem)
        keep.start()
        keep.wait()

    rounds = pl.cdiv(n, STEP)

    def out_copy(i, k):
        side = lax.rem(i, 2)
        to = jnp.minimum(i * STEP + k, KEPT)
        return pltpu.make_async_copy(bufs[k].at[side], tiles_ref.at[to], sem.at[side, k])

    def add_tile(code, k, side):
        t, held, b = decode(code)
        add_product(t, block_of(flux_ref, b), bufs[k][side], sum_ref)

    def step(i, carry):
        @pl.when(i >= 2)
        def _():
            for k in range(STEP):
                out_copy(i - 2, k).wait()

        side = lax.rem(i, 2)
        before = jnp.where(i > 0, list_ref[jnp.maximum(i * STEP - 1, 0)], SKIP)
        for k in range(STEP):
            code = list_ref[i * STEP + k]
            t, held, b = decode(code)
            build_tile(held, b, geo_ref, centre_ref, column_ref, offset_ref, bufs[k], side)
            if k == 0:
                add_tile(before, STEP - 1, 1 - side)
            else:
                add_tile(before, k - 1, side)
            before = code
        for k in range(STEP):
            out_copy(i, k).start()
        return carry

    lax.fori_loop(0, rounds, step, 0)
    last = jnp.where(rounds > 0, list_ref[jnp.maximum(rounds * STEP - 1, 0)], SKIP)
    add_tile(last, STEP - 1, lax.rem(rounds + 1, 2))
    for back in (2, 1):

        @pl.when(rounds >= back)
        def _():
            for k in range(STEP):
                out_copy(rounds - back, k).wait()

    for load in loads:
        load.wait()
    for u in range(16):
        lanes = slice(u * HALF, (u + 1) * HALF)
        reflect = reflect_of(table_ref, material_ref, lanes)
        radiosity = emission_ref[:, lanes] + reflect * sum_ref[u // 2, u % 2]
        area = geo_ref[first + u // 2, u % 2, 3:4, :]
        leaving_ref[u] = (area * radiosity).astype(jnp.bfloat16)


def second_kernel(
    list_ref, count_ref, geo_all, flux_ref, emission_ref, material_ref, table_ref, tiles_ref,
    out_ref,
    geo_ref, load_sem, centre_ref, column_ref, offset_ref, sum_ref, spare_ref, buf_ref, sem,
):
    n = count_ref[0]
    rounds = pl.cdiv(jnp.minimum(n, KEPT), STEP2)

    def in_copy(i):
        side = lax.rem(i, DEPTH)
        return pltpu.make_async_copy(
            tiles_ref.at[pl.ds(i * STEP2, STEP2)], buf_ref.at[side], sem.at[side]
        )

    for i in range(DEPTH - 1):

        @pl.when(i < rounds)
        def _():
            in_copy(i).start()

    sum_ref[...] = jnp.zeros_like(sum_ref)

    def step(i, carry):
        @pl.when(i + DEPTH - 1 < rounds)
        def _():
            in_copy(i + DEPTH - 1).start()

        in_copy(i).wait()
        side = lax.rem(i, DEPTH)
        for k in range(STEP2):
            t, held, b = decode(list_ref[i * STEP2 + k])
            add_product(t, block_of(flux_ref, b), buf_ref[side, k], sum_ref)
        return carry

    lax.fori_loop(0, rounds, step, 0)

    @pl.when(n > KEPT)
    def _():
        again_load = pltpu.make_async_copy(geo_all, geo_ref, load_sem)
        again_load.start()
        again_load.wait()
        prepare_targets(geo_ref, centre_ref, column_ref, offset_ref)

        def again(e, carry):
            t, held, b = decode(list_ref[e])
            build_tile(held, b, geo_ref, centre_ref, column_ref, offset_ref, spare_ref, 0)
            add_product(t, block_of(flux_ref, b), spare_ref[0], sum_ref)
            return carry

        lax.fori_loop(KEPT, n, again, 0)

    for u in range(16):
        lanes = slice(u * HALF, (u + 1) * HALF)
        reflect = reflect_of(table_ref, material_ref, lanes)
        out_ref[:, lanes] = emission_ref[:, lanes] + reflect * sum_ref[u // 2, u % 2]


def per_device(
    positions, normals, emission, material, area_level, reflect_table, area_table, pair_slots
):
    patches = positions.shape[1]
    units = patches // HALF
    peers = pair_slots.shape[1]
    blocks = peers * 8
    vmem = pl.BlockSpec(memory_space=pltpu.VMEM)
    smem = pl.BlockSpec(memory_space=pltpu.SMEM)
    anywhere = pl.BlockSpec(memory_space=pl.ANY)
    resident = pl.BlockSpec(memory_space=pltpu.HBM)
    material, level = material.reshape(1, patches), area_level.reshape(1, patches)
    slots = jnp.transpose(pair_slots[0], (1, 2, 0))
    pin = lambda x: pltpu.with_memory_space_constraint(x, pltpu.HBM)
    geo_units = jax.ShapeDtypeStruct((units, 8, HALF), jnp.float32)
    flux_units = jax.ShapeDtypeStruct((units, BANDS, HALF), jnp.bfloat16)
    geo, flux = gather_all(
        [geo_units, flux_units],
        FIRST_PARTS,
        0,
        [resident] * 6,
        [pin(x) for x in (positions, normals, emission, level, area_table.reshape(1, -1), slots)],
        own_first,
    )
    geo = geo.reshape(blocks, 2, 8, HALF)

    scratch = [
        pltpu.VMEM((8, 8, BLK), jnp.float32),
        pltpu.VMEM((8, 3 * BLK, 64), jnp.bfloat16),
        pltpu.VMEM((8, BLK, HALF), jnp.float32),
        pltpu.VMEM((9, 2, BANDS, HALF), jnp.float32),
    ]
    leaving, tiles, listed, counted, kept = pl.pallas_call(
        first_kernel,
        out_shape=[
            jax.ShapeDtypeStruct((units, BANDS, HALF), jnp.bfloat16),
            jax.ShapeDtypeStruct((KEPT + STEP2, BLK, BLK), jnp.bfloat16),
            jax.ShapeDtypeStruct((4 * peers + STEP2,), jnp.int32),
            jax.ShapeDtypeStruct((1,), jnp.int32),
            jax.ShapeDtypeStruct(geo.shape, jnp.float32),
        ],
        in_specs=[vmem] * 2 + [resident] * 3,
        out_specs=[vmem, anywhere, smem, smem, anywhere],
        scratch_shapes=[
            pltpu.VMEM(emission.shape, jnp.float32),
            pltpu.VMEM(material.shape, jnp.int32),
            pltpu.VMEM(reflect_table.shape, jnp.float32),
            pltpu.SemaphoreType.DMA((3,)),
            pltpu.VMEM((peers, HALF), jnp.float32),
            pltpu.VMEM((8, peers), jnp.int32),
            pltpu.SMEM((8, peers), jnp.int32),
            pltpu.SemaphoreType.DMA(()),
        ]
        + scratch
        + [pltpu.VMEM((2, BLK, BLK), jnp.bfloat16)] * STEP
        + [pltpu.SemaphoreType.DMA((2, STEP))],
        compiler_params=pltpu.CompilerParams(vmem_limit_bytes=20 << 20),
        name="first_sweep",
    )(geo, flux.reshape(blocks, 2, BANDS, HALF), pin(emission), pin(material), pin(reflect_table))
    (flux,) = gather_all([flux_units], LATER_PARTS, 1, [anywhere], [leaving])
    return pl.pallas_call(
        second_kernel,
        out_shape=jax.ShapeDtypeStruct((BANDS, patches), jnp.float32),
        in_specs=[smem, smem, anywhere] + [vmem] * 4 + [anywhere],
        out_specs=vmem,
        scratch_shapes=[
            pltpu.VMEM((blocks, 2, 8, HALF), jnp.float32),
            pltpu.SemaphoreType.DMA(()),
        ]
        + scratch
        + [
            pltpu.VMEM((1, BLK, BLK), jnp.bfloat16),
            pltpu.VMEM((DEPTH, STEP2, BLK, BLK), jnp.bfloat16),
            pltpu.SemaphoreType.DMA((DEPTH,)),
        ],
        compiler_params=pltpu.CompilerParams(vmem_limit_bytes=34 << 20),
        name="second_sweep",
    )(
        listed, counted, kept, flux.reshape(blocks, 2, BANDS, HALF), emission, material,
        reflect_table, tiles,
    )


def solution(mesh):
    placed = (
        P(None, AXES),
        P(None, AXES),
        P(None, AXES),
        P(AXES),
        P(AXES),
        P(),
        P(),
        P(AXES, None, None, None),
    )
    return jax.shard_map(
        per_device, mesh=mesh, in_specs=placed, out_specs=P(None, AXES), check_vma=False
    )
```

```python
import functools
import math

import jax
import jax.numpy as jnp
from jax import lax
from jax.experimental import pallas as pl
from jax.experimental.pallas import tpu as pltpu
from jax.sharding import PartitionSpec as P

MESH = pl.DeviceIdType.MESH
BANDS = 16
BLK = 256
HALF = 128
ITERS = 2
AXES = ("gx", "gy")
SIDE = 4
ORDERS = (("x", "y", "z"), ("y", "z", "x"), ("z", "x", "y"))
FIRST_PARTS = (((0, 11), (1, 5)), ((1, 6), (2, 10)))
LATER_PARTS = (((0, 6), (1, 5), (2, 5)),)
KEPT = 336
STEP = 16
STEP2 = 16
TAIL = 4
CHUNK = 64
DEPTH = 4
SKIP = 8 << 10
KAPPA = (math.pi - 1.0) / math.pi


def my_place():
    z = lax.axis_index("gx")
    inner = lax.axis_index("gy")
    place = {"z": z, "y": lax.div(inner, 2 * SIDE), "x": lax.rem(lax.div(inner, 2), SIDE)}
    return place, lax.rem(inner, 2)


def device_of(place, core):
    return (place["z"], (place["y"] * SIDE + place["x"]) * 2 + core)


def moved(place, axis, by):
    other = dict(place)
    other[axis] = lax.rem(place[axis] + (by + SIDE), SIDE)
    return other


def own_first(refs, srcs):
    geo_ref, flux_ref, *held, load_sem = srcs
    loads = [
        pltpu.make_async_copy(ref, to, load_sem.at[n]) for n, (ref, to) in enumerate(zip(refs, held))
    ]
    for load in loads:
        load.start()
    for load in loads:
        load.wait()
    position_ref, normal_ref, emission_ref, level_ref, area_ref, slot_ref = held
    for u in range(position_ref.shape[1] // HALF):
        lanes = slice(u * HALF, (u + 1) * HALF)
        level = level_ref[:, lanes]
        area = jnp.zeros(level.shape, jnp.float32)
        for m in range(area_ref.shape[1]):
            area = jnp.where(level == m, area_ref[0:1, m : m + 1], area)
        code = jnp.zeros(area.shape, jnp.float32)
        if u < 2:
            row, column = slot_ref[u, 0:1, :], slot_ref[u, 1:2, :]
            code = jnp.where(row >= 0, row * 8 + column, -1).astype(jnp.float32)
        geo_ref[u] = jnp.concatenate(
            [position_ref[:, lanes], area, normal_ref[:, lanes], code], axis=0
        )
        flux_ref[u] = (area * emission_ref[:, lanes]).astype(jnp.bfloat16)


def gather_kernel(parts, count, prologue, inputs, short, *refs):
    bufs, rest = refs[inputs : inputs + count], refs[inputs + count :]
    send_sem, recv_sem, local_sem = rest[:3]
    srcs = rest[3:] if prologue else refs[:count]
    here, core = my_place()
    other_core = device_of(here, 1 - core)
    barrier = pltpu.get_barrier_semaphore()
    peers = [device_of(moved(here, axis, by), core) for axis in "zyx" for by in (1, -1, 2)]
    peers.append(other_core)
    for peer in peers:
        pl.semaphore_signal(barrier, inc=1, device_id=peer, device_id_type=MESH)
    if prologue:
        prologue(refs[:inputs], srcs)
    own_copies = []
    for b in range(count):
        place = bufs[b].at[here["z"], here["y"], here["x"], core]
        own_copies.append(pltpu.make_async_copy(srcs[b], place, local_sem.at[b]))
        own_copies[-1].start()
    pl.semaphore_wait(barrier, len(peers))
    started = []
    shared = []

    def send(src, dst, to):
        n = len(started)
        copy = pltpu.make_async_remote_copy(
            src_ref=src,
            dst_ref=dst,
            send_sem=send_sem.at[n],
            recv_sem=recv_sem.at[n],
            device_id=to,
            device_id_type=MESH,
        )
        copy.start()
        started.append(copy)
        return copy

    def view(b, index, first, size):
        return bufs[b].at[index["z"], index["y"], index["x"], core, pl.ds(first, size)]

    def share(b, index, first, size):
        piece = view(b, index, first, size)
        shared.append(send(piece, piece, other_core))

    work = []
    for b in range(count):
        first = 0
        for k, size in parts[b]:
            work.append((b, k, first, size))
            first += size

    for copy in own_copies:
        copy.wait()

    def at(k, line, plane, far):
        index = {}
        for axis, by in zip(ORDERS[k], (line, plane, far)):
            index[axis] = pl.ds(0, SIDE) if by is None else moved(here, axis, by)[axis]
        return index

    def to(k, stage, by):
        return device_of(moved(here, ORDERS[k][stage], by), core)

    def pass_on(item, stage, by, index):
        b, k, first, size = item
        piece = view(b, index, first, size)
        return send(piece, piece, to(k, stage, by))

    def half(k, index, which):
        index = dict(index)
        index[ORDERS[k][0]] = pl.ds(2 * which, 2)
        return index

    line, plane, ahead, far, again = {}, {}, {}, {}, {}
    for item in work:
        b, k, first, size = item
        src, dst = srcs[b].at[pl.ds(first, size)], view(b, here, first, size)
        line[item] = [send(src, dst, to(k, 0, by)) for by in (1, -1, 2)]
    for item in work:
        b, k, first, size = item
        for copy in line[item]:
            copy.wait_recv()
        mine = at(k, None, 0, 0)
        steps = (1, -1, 2) if short else (1, -1)
        plane[item] = {by: pass_on(item, 1, by, mine) for by in steps}
        for by in (1, -1):
            far[item, 0, by] = pass_on(item, 2, by, mine)
        share(b, mine, first, size)
    for item in work:
        b, k, first, size = item
        if short:
            ahead[item] = [plane[item][2]]
        else:
            plane[item][1].wait_recv()
            up = pass_on(item, 1, 1, half(k, at(k, None, -1, 0), 0))
            plane[item][-1].wait_recv()
            down = pass_on(item, 1, -1, half(k, at(k, None, 1, 0), 1))
            ahead[item] = [up, down]
        for row in (-1, 1):
            if short:
                plane[item][-row].wait_recv()
            index = at(k, None, row, 0)
            for by in (1, -1):
                far[item, row, by] = pass_on(item, 2, by, index)
            share(b, index, first, size)

    def forward(item, row):
        k = item[1]
        far[item, row, 1].wait_recv()
        if short and row == 2:
            far[item, row, -1].wait_recv()
            again[item, row] = [far[item, row, 2]]
            return
        up = pass_on(item, 2, 1, half(k, at(k, None, row, -1), 0))
        far[item, row, -1].wait_recv()
        down = pass_on(item, 2, -1, half(k, at(k, None, row, 1), 1))
        again[item, row] = [up, down]

    def share_far(item, row):
        b, k, first, size = item
        share(b, at(k, None, row, -1), first, size)
        share(b, at(k, None, row, 1), first, size)

    for item in work:
        forward(item, 0)
        share_far(item, 0)
    for item in work:
        b, k, first, size = item
        for copy in ahead[item]:
            copy.wait_recv()
        index = at(k, None, 2, 0)
        for by in (1, -1, 2) if short else (1, -1):
            far[item, 2, by] = pass_on(item, 2, by, index)
        share(b, index, first, size)
    for row in (-1, 1, 2):
        for item in work:
            forward(item, row)
            share_far(item, row)
    for row in (0, -1, 1, 2):
        for item in work:
            b, k, first, size = item
            for copy in again[item, row]:
                copy.wait_recv()
            share(b, at(k, None, row, 2), first, size)
    for copy in shared:
        copy.wait_recv()
    for copy in started:
        copy.wait_send()


def gather_all(shapes, parts, collective_id, specs, inputs, prologue=None, short=False):
    count = len(shapes)
    copies = 39 * sum(len(p) for p in parts)
    own = []
    if prologue:
        own = [pltpu.VMEM(a.shape, a.dtype) for a in list(shapes) + list(inputs)]
        own.append(pltpu.SemaphoreType.DMA((len(inputs),)))
    return pl.pallas_call(
        functools.partial(gather_kernel, parts, count, prologue, len(inputs), short),
        out_shape=[
            jax.ShapeDtypeStruct((SIDE, SIDE, SIDE, 2) + a.shape, a.dtype) for a in shapes
        ],
        in_specs=specs,
        out_specs=[pl.BlockSpec(memory_space=pl.ANY)] * count,
        scratch_shapes=[
            pltpu.SemaphoreType.DMA((copies,)),
            pltpu.SemaphoreType.DMA((copies,)),
            pltpu.SemaphoreType.DMA((count,)),
        ]
        + own,
        compiler_params=pltpu.CompilerParams(
            collective_id=collective_id, has_side_effects=True, vmem_limit_bytes=2 << 20
        ),
        name="gather_all",
    )(*inputs)


def my_block():
    return (lax.axis_index("gx") * lax.axis_size("gy") + lax.axis_index("gy")) * 8


def reflect_of(table_ref, material_ref, lanes):
    material = material_ref[:, lanes]
    kinds = table_ref.shape[0]
    hot = lax.broadcasted_iota(jnp.int32, (kinds, HALF), 0) == material
    return lax.dot_general(
        table_ref[...],
        jnp.where(hot, 1.0, 0.0),
        (((0,), (0,)), ((), ())),
        precision=lax.Precision.HIGHEST,
        preferred_element_type=jnp.float32,
    )


def split3(x):
    a = x.astype(jnp.bfloat16).astype(jnp.float32)
    rest = x - a
    b = rest.astype(jnp.bfloat16).astype(jnp.float32)
    return a, b, rest - b


def block_of(ref, b):
    return jnp.concatenate([ref[b, 0], ref[b, 1]], axis=1)


def centred(rows, centre):
    moved_rows = rows - centre
    squares = moved_rows * moved_rows
    cross = moved_rows * pltpu.roll(moved_rows, 4, 0)
    reach = (squares[0:1] + squares[1:2] + squares[2:3]) + 0.5 * rows[3:4]
    plane = -(cross[0:1] + cross[1:2] + cross[2:3])
    return moved_rows, reach, plane


def source_rows(rows, centre):
    at = lax.broadcasted_iota(jnp.int32, rows.shape, 0)
    base, reach, plane = centred(rows, centre)
    base = jnp.where(at == 3, reach, jnp.where(at == 7, plane, base))
    a, b, c = split3(base)
    one = jnp.where(at < 3, 1.0, 0.0)
    stacked = jnp.concatenate([a, a, a, b, b, c, one, jnp.zeros_like(one)], axis=0)
    return stacked.astype(jnp.bfloat16), (KAPPA * 0.5) * rows[3:4]


def target_columns(rows, centre):
    at = lax.broadcasted_iota(jnp.int32, rows.shape, 0)
    base, reach, plane = centred(rows, centre)
    zero = jnp.zeros_like(base)
    swapped = pltpu.roll(base, 4, 0)
    facing = jnp.where(at < 3, swapped, 0.0) * (1.0 / math.pi)
    seen = jnp.where((at >= 4) & (at < 7), swapped, jnp.where(at == 7, 1.0, 0.0))
    spread = jnp.where(at < 3, -2.0 * base, jnp.where(at == 3, 1.0, 0.0))
    columns = []
    for factor, constant in ((facing, plane * (1.0 / math.pi)), (seen, None), (spread, reach)):
        a, b, c = split3(factor)
        last = zero
        if constant is not None:
            d, e, f = split3(constant)
            last = jnp.where(at == 0, d, jnp.where(at == 1, e, jnp.where(at == 2, f, 0.0)))
        stacked = jnp.concatenate([a, b, c, a, b, a, last, zero], axis=0)
        columns.append(jnp.transpose(stacked).astype(jnp.bfloat16))
    return columns, (KAPPA * 0.5) * rows[3:4]


def prepare_targets(geo_ref, centre_ref, column_ref, offset_ref):
    for t in range(8):
        rows = block_of(geo_ref, my_block() + t)
        at = lax.broadcasted_iota(jnp.int32, rows.shape, 0)
        centre = jnp.where(at < 3, jnp.broadcast_to(rows[:, 0:1], rows.shape), 0.0)
        centre_ref[t] = centre
        columns, offset = target_columns(rows, centre)
        for r in range(0, BLK, CHUNK):
            column_ref[t, 3 * r : 3 * (r + CHUNK)] = jnp.concatenate(
                [c[r : r + CHUNK] for c in columns], axis=0
            )
        offset_ref[t] = jnp.transpose(jnp.broadcast_to(offset, (HALF, BLK)))


def build_tile(t, b, geo_ref, centre_ref, column_ref, offset_ref, tile_ref, slot):
    source, source_offset = source_rows(block_of(geo_ref, b), centre_ref[t])
    for r in range(0, BLK, CHUNK):
        terms = jnp.dot(
            column_ref[t, 3 * r : 3 * (r + CHUNK), :], source, preferred_element_type=jnp.float32
        )
        facing, seen, spread = terms[:CHUNK], terms[CHUNK : 2 * CHUNK], terms[2 * CHUNK :]
        offset = offset_ref[t, r : r + CHUNK, :]
        offset = jnp.concatenate([offset, offset], axis=1)
        over = jnp.maximum(facing, 0.0) * jnp.maximum(seen, 0.0)
        under = spread * ((spread - offset) - source_offset)
        tile_ref[slot, r : r + CHUNK, :] = (over / under).astype(jnp.bfloat16)


def add_product(t, flux, tile, sum_ref):
    term = lax.dot_general(
        flux, tile, (((1,), (1,)), ((), ())), preferred_element_type=jnp.float32
    )
    sum_ref[t, 0] += term[:, :HALF]
    sum_ref[t, 1] += term[:, HALF:]


def decode(code):
    t = lax.shift_right_logical(code, 10)
    return t, jnp.minimum(t, 7), lax.bitwise_and(code, 1023)


def first_kernel(
    geo_ref, flux_ref, emission_all, material_all, table_all,
    leaving_ref, tiles_ref, list_ref, count_ref, kept_ref,
    emission_ref, material_ref, table_ref, load_sem, code_ref, entry_ref, slot_ref, slot_sem, centre_ref, column_ref, offset_ref, sum_ref, *rest,
):
    bufs, sem = rest[:STEP], rest[STEP]
    loads = [
        pltpu.make_async_copy(emission_all, emission_ref, load_sem.at[0]),
        pltpu.make_async_copy(material_all, material_ref, load_sem.at[1]),
        pltpu.make_async_copy(table_all, table_ref, load_sem.at[2]),
    ]
    for load in loads:
        load.start()
    first = my_block()
    peers = geo_ref.shape[0] // 8
    peer = lax.broadcasted_iota(jnp.int32, (1, peers), 1)
    at_me = lax.broadcasted_iota(jnp.int32, (8, HALF), 1) == lax.div(first, 8)
    pick = jnp.where(at_me, 1.0, 0.0).astype(jnp.bfloat16)
    entry_ref[...] = jnp.full_like(entry_ref, -1)
    for c in range(2):
        for p in range(peers):
            code_ref[p : p + 1, :] = geo_ref[p * 8, c, 7:8, :]
        served = lax.dot_general(
            pick,
            code_ref[...].astype(jnp.bfloat16),
            (((1,), (1,)), ((), ())),
            preferred_element_type=jnp.float32,
        )[0:1].astype(jnp.int32)
        owned = geo_ref[first, c, 7:8, :].astype(jnp.int32)
        for row, code, own in ((c, owned, True), (2 + c, served, False)):
            high, low = lax.shift_right_arithmetic(code, 3), lax.bitwise_and(code, 7)
            target, source = (high, low) if own else (low, high)
            entry_ref[row : row + 1, :] = jnp.where(
                code >= 0, target * 1024 + peer * 8 + source, -1
            )
    slot_copy = pltpu.make_async_copy(entry_ref, slot_ref, slot_sem)
    slot_copy.start()
    prepare_targets(geo_ref, centre_ref, column_ref, offset_ref)
    sum_ref[...] = jnp.zeros_like(sum_ref)
    slot_copy.wait()
    bufs[-1][1] = jnp.zeros_like(bufs[-1][1])

    def compact(e, n):
        for k in range(8):
            code = slot_ref[lax.div(e, HALF // 8), lax.rem(e, HALF // 8) * 8 + k]
            list_ref[n] = code
            n = n + jnp.where(code >= 0, 1, 0)
        return n

    n = lax.fori_loop(0, 4 * HALF // 8, compact, 0)
    for k in range(STEP2):
        list_ref[n + k] = SKIP
    count_ref[0] = n

    @pl.when(n > KEPT)
    def _():
        keep = pltpu.make_async_copy(geo_ref, kept_ref, slot_sem)
        keep.start()
        keep.wait()

    rounds = lax.div(n, STEP)
    rest = n - rounds * STEP

    def out_copy(i, k):
        side = lax.rem(i, 2)
        to = jnp.minimum(i * STEP + k, KEPT)
        return pltpu.make_async_copy(bufs[k].at[side], tiles_ref.at[to], sem.at[side, k])

    def add_tile(code, k, side):
        t, held, b = decode(code)
        add_product(t, block_of(flux_ref, b), bufs[k][side], sum_ref)

    def step(i, carry):
        @pl.when(i >= 2)
        def _():
            for k in range(STEP):
                out_copy(i - 2, k).wait()

        side = lax.rem(i, 2)
        before = jnp.where(i > 0, list_ref[jnp.maximum(i * STEP - 1, 0)], SKIP)
        for k in range(STEP):
            code = list_ref[i * STEP + k]
            t, held, b = decode(code)
            build_tile(held, b, geo_ref, centre_ref, column_ref, offset_ref, bufs[k], side)
            if k == 0:
                add_tile(before, STEP - 1, 1 - side)
            else:
                add_tile(before, k - 1, side)
            before = code
        for k in range(STEP):
            out_copy(i, k).start()
        return carry

    lax.fori_loop(0, rounds, step, 0)
    last = jnp.where(rounds > 0, list_ref[jnp.maximum(rounds * STEP - 1, 0)], SKIP)
    add_tile(last, STEP - 1, lax.rem(rounds + 1, 2))

    @pl.when(rounds >= 2)
    def _():
        for k in range(STEP):
            out_copy(rounds - 2, k).wait()

    side = lax.rem(rounds, 2)
    for low in range(0, STEP, TAIL):

        @pl.when(rest > low)
        def _():
            codes = [list_ref[rounds * STEP + k] for k in range(low, low + TAIL)]
            for k in range(low, low + TAIL):
                t, held, b = decode(codes[k - low])
                build_tile(held, b, geo_ref, centre_ref, column_ref, offset_ref, bufs[k], side)
                if k > low:
                    add_tile(codes[k - low - 1], k - 1, side)
                out_copy(rounds, k).start()
            add_tile(codes[-1], low + TAIL - 1, side)

    @pl.when(rounds >= 1)
    def _():
        for k in range(STEP):
            out_copy(rounds - 1, k).wait()

    for low in range(0, STEP, TAIL):

        @pl.when(rest > low)
        def _():
            for k in range(low, low + TAIL):
                out_copy(rounds, k).wait()

    for load in loads:
        load.wait()
    for u in range(16):
        lanes = slice(u * HALF, (u + 1) * HALF)
        reflect = reflect_of(table_ref, material_ref, lanes)
        radiosity = emission_ref[:, lanes] + reflect * sum_ref[u // 2, u % 2]
        area = geo_ref[first + u // 2, u % 2, 3:4, :]
        leaving_ref[u] = (area * radiosity).astype(jnp.bfloat16)


def second_kernel(
    list_ref, count_ref, geo_all, flux_ref, emission_ref, material_ref, table_ref, tiles_ref,
    out_ref,
    geo_ref, load_sem, centre_ref, column_ref, offset_ref, sum_ref, spare_ref, buf_ref, sem,
):
    n = count_ref[0]
    rounds = pl.cdiv(jnp.minimum(n, KEPT), STEP2)

    def in_copy(i):
        side = lax.rem(i, DEPTH)
        return pltpu.make_async_copy(
            tiles_ref.at[pl.ds(i * STEP2, STEP2)], buf_ref.at[side], sem.at[side]
        )

    for i in range(DEPTH - 1):

        @pl.when(i < rounds)
        def _():
            in_copy(i).start()

    sum_ref[...] = jnp.zeros_like(sum_ref)

    def step(i, carry):
        @pl.when(i + DEPTH - 1 < rounds)
        def _():
            in_copy(i + DEPTH - 1).start()

        in_copy(i).wait()
        side = lax.rem(i, DEPTH)
        for k in range(STEP2):
            t, held, b = decode(list_ref[i * STEP2 + k])
            add_product(t, block_of(flux_ref, b), buf_ref[side, k], sum_ref)
        return carry

    lax.fori_loop(0, rounds, step, 0)

    @pl.when(n > KEPT)
    def _():
        again_load = pltpu.make_async_copy(geo_all, geo_ref, load_sem)
        again_load.start()
        again_load.wait()
        prepare_targets(geo_ref, centre_ref, column_ref, offset_ref)

        def again(e, carry):
            t, held, b = decode(list_ref[e])
            build_tile(held, b, geo_ref, centre_ref, column_ref, offset_ref, spare_ref, 0)
            add_product(t, block_of(flux_ref, b), spare_ref[0], sum_ref)
            return carry

        lax.fori_loop(KEPT, n, again, 0)

    for u in range(16):
        lanes = slice(u * HALF, (u + 1) * HALF)
        reflect = reflect_of(table_ref, material_ref, lanes)
        out_ref[:, lanes] = emission_ref[:, lanes] + reflect * sum_ref[u // 2, u % 2]


def per_device(
    positions, normals, emission, material, area_level, reflect_table, area_table, pair_slots
):
    patches = positions.shape[1]
    units = patches // HALF
    peers = pair_slots.shape[1]
    blocks = peers * 8
    vmem = pl.BlockSpec(memory_space=pltpu.VMEM)
    smem = pl.BlockSpec(memory_space=pltpu.SMEM)
    anywhere = pl.BlockSpec(memory_space=pl.ANY)
    resident = pl.BlockSpec(memory_space=pltpu.HBM)
    material, level = material.reshape(1, patches), area_level.reshape(1, patches)
    slots = jnp.transpose(pair_slots[0], (1, 2, 0))
    pin = lambda x: pltpu.with_memory_space_constraint(x, pltpu.HBM)
    geo_units = jax.ShapeDtypeStruct((units, 8, HALF), jnp.float32)
    flux_units = jax.ShapeDtypeStruct((units, BANDS, HALF), jnp.bfloat16)
    geo, flux = gather_all(
        [geo_units, flux_units],
        FIRST_PARTS,
        0,
        [resident] * 6,
        [pin(x) for x in (positions, normals, emission, level, area_table.reshape(1, -1), slots)],
        own_first,
    )
    geo = geo.reshape(blocks, 2, 8, HALF)

    scratch = [
        pltpu.VMEM((8, 8, BLK), jnp.float32),
        pltpu.VMEM((8, 3 * BLK, 64), jnp.bfloat16),
        pltpu.VMEM((8, BLK, HALF), jnp.float32),
        pltpu.VMEM((9, 2, BANDS, HALF), jnp.float32),
    ]
    leaving, tiles, listed, counted, kept = pl.pallas_call(
        first_kernel,
        out_shape=[
            jax.ShapeDtypeStruct((units, BANDS, HALF), jnp.bfloat16),
            jax.ShapeDtypeStruct((KEPT + STEP2, BLK, BLK), jnp.bfloat16),
            jax.ShapeDtypeStruct((4 * peers + STEP2,), jnp.int32),
            jax.ShapeDtypeStruct((1,), jnp.int32),
            jax.ShapeDtypeStruct(geo.shape, jnp.float32),
        ],
        in_specs=[vmem] * 2 + [resident] * 3,
        out_specs=[vmem, anywhere, smem, smem, anywhere],
        scratch_shapes=[
            pltpu.VMEM(emission.shape, jnp.float32),
            pltpu.VMEM(material.shape, jnp.int32),
            pltpu.VMEM(reflect_table.shape, jnp.float32),
            pltpu.SemaphoreType.DMA((3,)),
            pltpu.VMEM((peers, HALF), jnp.float32),
            pltpu.VMEM((8, peers), jnp.int32),
            pltpu.SMEM((8, peers), jnp.int32),
            pltpu.SemaphoreType.DMA(()),
        ]
        + scratch
        + [pltpu.VMEM((2, BLK, BLK), jnp.bfloat16)] * STEP
        + [pltpu.SemaphoreType.DMA((2, STEP))],
        compiler_params=pltpu.CompilerParams(vmem_limit_bytes=20 << 20),
        name="first_sweep",
    )(geo, flux.reshape(blocks, 2, BANDS, HALF), pin(emission), pin(material), pin(reflect_table))
    (flux,) = gather_all(
        [flux_units], LATER_PARTS, 1, [anywhere], [leaving], short=True
    )
    return pl.pallas_call(
        second_kernel,
        out_shape=jax.ShapeDtypeStruct((BANDS, patches), jnp.float32),
        in_specs=[smem, smem, anywhere] + [vmem] * 4 + [anywhere],
        out_specs=vmem,
        scratch_shapes=[
            pltpu.VMEM((blocks, 2, 8, HALF), jnp.float32),
            pltpu.SemaphoreType.DMA(()),
        ]
        + scratch
        + [
            pltpu.VMEM((1, BLK, BLK), jnp.bfloat16),
            pltpu.VMEM((DEPTH, STEP2, BLK, BLK), jnp.bfloat16),
            pltpu.SemaphoreType.DMA((DEPTH,)),
        ],
        compiler_params=pltpu.CompilerParams(vmem_limit_bytes=34 << 20),
        name="second_sweep",
    )(
        listed, counted, kept, flux.reshape(blocks, 2, BANDS, HALF), emission, material,
        reflect_table, tiles,
    )


def solution(mesh):
    placed = (
        P(None, AXES),
        P(None, AXES),
        P(None, AXES),
        P(AXES),
        P(AXES),
        P(),
        P(),
        P(AXES, None, None, None),
    )
    return jax.shard_map(
        per_device, mesh=mesh, in_specs=placed, out_specs=P(None, AXES), check_vma=False
    )
```

```python
import functools
import math

import jax
import jax.numpy as jnp
from jax import lax
from jax.experimental import pallas as pl
from jax.experimental.pallas import tpu as pltpu
from jax.sharding import PartitionSpec as P

MESH = pl.DeviceIdType.MESH
BANDS = 16
BLK = 256
HALF = 128
ITERS = 2
AXES = ("gx", "gy")
SIDE = 4
ORDERS = (("x", "y", "z"), ("y", "z", "x"), ("z", "x", "y"))
FIRST_PARTS = (((0, 11), (1, 5)), ((1, 6), (2, 10)))
LATER_PARTS = (((0, 6), (1, 5), (2, 5)),)
KEPT = 336
STEP = 16
STEP2 = 16
TAIL = 4
CHUNK = 64
DEPTH = 4
SKIP = 8 << 10
KAPPA = (math.pi - 1.0) / math.pi


def my_place():
    z = lax.axis_index("gx")
    inner = lax.axis_index("gy")
    place = {"z": z, "y": lax.div(inner, 2 * SIDE), "x": lax.rem(lax.div(inner, 2), SIDE)}
    return place, lax.rem(inner, 2)


def device_of(place, core):
    return (place["z"], (place["y"] * SIDE + place["x"]) * 2 + core)


def moved(place, axis, by):
    other = dict(place)
    other[axis] = lax.rem(place[axis] + (by + SIDE), SIDE)
    return other


def own_first(refs, srcs):
    geo_ref, flux_ref, *held, load_sem = srcs
    loads = [
        pltpu.make_async_copy(ref, to, load_sem.at[n]) for n, (ref, to) in enumerate(zip(refs, held))
    ]
    for load in loads:
        load.start()
    for load in loads:
        load.wait()
    position_ref, normal_ref, emission_ref, level_ref, area_ref, slot_ref = held
    for u in range(position_ref.shape[1] // HALF):
        lanes = slice(u * HALF, (u + 1) * HALF)
        level = level_ref[:, lanes]
        area = jnp.zeros(level.shape, jnp.float32)
        for m in range(area_ref.shape[1]):
            area = jnp.where(level == m, area_ref[0:1, m : m + 1], area)
        code = jnp.zeros(area.shape, jnp.float32)
        if u < 2:
            row, column = slot_ref[u, 0:1, :], slot_ref[u, 1:2, :]
            code = jnp.where(row >= 0, row * 8 + column, -1).astype(jnp.float32)
        geo_ref[u] = jnp.concatenate(
            [position_ref[:, lanes], area, normal_ref[:, lanes], code], axis=0
        )
        flux_ref[u] = (area * emission_ref[:, lanes]).astype(jnp.bfloat16)


def gather_kernel(parts, count, prologue, inputs, short, *refs):
    bufs, rest = refs[inputs : inputs + count], refs[inputs + count :]
    send_sem, recv_sem, local_sem = rest[:3]
    srcs = rest[3:] if prologue else refs[:count]
    here, core = my_place()
    other_core = device_of(here, 1 - core)
    barrier = pltpu.get_barrier_semaphore()
    peers = [device_of(moved(here, axis, by), core) for axis in "zyx" for by in (1, -1, 2)]
    peers.append(other_core)
    for peer in peers:
        pl.semaphore_signal(barrier, inc=1, device_id=peer, device_id_type=MESH)
    if prologue:
        prologue(refs[:inputs], srcs)
    own_copies = []
    for b in range(count):
        place = bufs[b].at[here["z"], here["y"], here["x"], core]
        own_copies.append(pltpu.make_async_copy(srcs[b], place, local_sem.at[b]))
        own_copies[-1].start()
    pl.semaphore_wait(barrier, len(peers))
    started = []
    shared = []

    def send(src, dst, to):
        n = len(started)
        copy = pltpu.make_async_remote_copy(
            src_ref=src,
            dst_ref=dst,
            send_sem=send_sem.at[n],
            recv_sem=recv_sem.at[n],
            device_id=to,
            device_id_type=MESH,
        )
        copy.start()
        started.append(copy)
        return copy

    def view(b, index, first, size):
        return bufs[b].at[index["z"], index["y"], index["x"], core, pl.ds(first, size)]

    def share(b, index, first, size):
        piece = view(b, index, first, size)
        shared.append(send(piece, piece, other_core))

    work = []
    for b in range(count):
        first = 0
        for k, size in parts[b]:
            work.append((b, k, first, size))
            first += size

    for copy in own_copies:
        copy.wait()

    def at(k, line, plane, far):
        index = {}
        for axis, by in zip(ORDERS[k], (line, plane, far)):
            index[axis] = pl.ds(0, SIDE) if by is None else moved(here, axis, by)[axis]
        return index

    def to(k, stage, by):
        return device_of(moved(here, ORDERS[k][stage], by), core)

    def pass_on(item, stage, by, index):
        b, k, first, size = item
        piece = view(b, index, first, size)
        return send(piece, piece, to(k, stage, by))

    def half(k, index, which):
        index = dict(index)
        index[ORDERS[k][0]] = pl.ds(2 * which, 2)
        return index

    line, plane, ahead, far, again = {}, {}, {}, {}, {}
    for item in work:
        b, k, first, size = item
        src, dst = srcs[b].at[pl.ds(first, size)], view(b, here, first, size)
        line[item] = [send(src, dst, to(k, 0, by)) for by in (1, -1, 2)]
    for item in work:
        b, k, first, size = item
        for copy in line[item]:
            copy.wait_recv()
        mine = at(k, None, 0, 0)
        steps = (1, -1, 2) if short else (1, -1)
        plane[item] = {by: pass_on(item, 1, by, mine) for by in steps}
        for by in (1, -1):
            far[item, 0, by] = pass_on(item, 2, by, mine)
        share(b, mine, first, size)
    for item in work:
        b, k, first, size = item
        if short:
            ahead[item] = [plane[item][2]]
        else:
            plane[item][1].wait_recv()
            up = pass_on(item, 1, 1, half(k, at(k, None, -1, 0), 0))
            plane[item][-1].wait_recv()
            down = pass_on(item, 1, -1, half(k, at(k, None, 1, 0), 1))
            ahead[item] = [up, down]
        for row in (-1, 1):
            if short:
                plane[item][-row].wait_recv()
            index = at(k, None, row, 0)
            for by in (1, -1):
                far[item, row, by] = pass_on(item, 2, by, index)
            share(b, index, first, size)

    def forward(item, row):
        k = item[1]
        far[item, row, 1].wait_recv()
        if short and row == 2:
            far[item, row, -1].wait_recv()
            again[item, row] = [far[item, row, 2]]
            return
        up = pass_on(item, 2, 1, half(k, at(k, None, row, -1), 0))
        far[item, row, -1].wait_recv()
        down = pass_on(item, 2, -1, half(k, at(k, None, row, 1), 1))
        again[item, row] = [up, down]

    def share_far(item, row):
        b, k, first, size = item
        share(b, at(k, None, row, -1), first, size)
        share(b, at(k, None, row, 1), first, size)

    for item in work:
        forward(item, 0)
        share_far(item, 0)
    for item in work:
        b, k, first, size = item
        for copy in ahead[item]:
            copy.wait_recv()
        index = at(k, None, 2, 0)
        for by in (1, -1, 2) if short else (1, -1):
            far[item, 2, by] = pass_on(item, 2, by, index)
        share(b, index, first, size)
    for row in (-1, 1, 2):
        for item in work:
            forward(item, row)
            share_far(item, row)
    for row in (0, -1, 1, 2):
        for item in work:
            b, k, first, size = item
            for copy in again[item, row]:
                copy.wait_recv()
            share(b, at(k, None, row, 2), first, size)
    for copy in shared:
        copy.wait_recv()
    for copy in started:
        copy.wait_send()


def gather_all(shapes, parts, collective_id, specs, inputs, prologue=None, short=False):
    count = len(shapes)
    copies = 39 * sum(len(p) for p in parts)
    own = []
    if prologue:
        own = [pltpu.VMEM(a.shape, a.dtype) for a in list(shapes) + list(inputs)]
        own.append(pltpu.SemaphoreType.DMA((len(inputs),)))
    return pl.pallas_call(
        functools.partial(gather_kernel, parts, count, prologue, len(inputs), short),
        out_shape=[
            jax.ShapeDtypeStruct((SIDE, SIDE, SIDE, 2) + a.shape, a.dtype) for a in shapes
        ],
        in_specs=specs,
        out_specs=[pl.BlockSpec(memory_space=pl.ANY)] * count,
        scratch_shapes=[
            pltpu.SemaphoreType.DMA((copies,)),
            pltpu.SemaphoreType.DMA((copies,)),
            pltpu.SemaphoreType.DMA((count,)),
        ]
        + own,
        compiler_params=pltpu.CompilerParams(
            collective_id=collective_id, has_side_effects=True, vmem_limit_bytes=2 << 20
        ),
        name="gather_all",
    )(*inputs)


def my_block():
    return (lax.axis_index("gx") * lax.axis_size("gy") + lax.axis_index("gy")) * 8


def reflect_of(table_ref, material_ref, lanes):
    material = material_ref[:, lanes]
    kinds = table_ref.shape[0]
    hot = lax.broadcasted_iota(jnp.int32, (kinds, HALF), 0) == material
    return lax.dot_general(
        table_ref[...],
        jnp.where(hot, 1.0, 0.0),
        (((0,), (0,)), ((), ())),
        precision=lax.Precision.HIGHEST,
        preferred_element_type=jnp.float32,
    )


def split3(x):
    a = x.astype(jnp.bfloat16).astype(jnp.float32)
    rest = x - a
    b = rest.astype(jnp.bfloat16).astype(jnp.float32)
    return a, b, rest - b


def block_of(ref, b):
    return jnp.concatenate([ref[b, 0], ref[b, 1]], axis=1)


def centred(rows, centre):
    moved_rows = rows - centre
    squares = moved_rows * moved_rows
    cross = moved_rows * pltpu.roll(moved_rows, 4, 0)
    reach = (squares[0:1] + squares[1:2] + squares[2:3]) + 0.5 * rows[3:4]
    plane = -(cross[0:1] + cross[1:2] + cross[2:3])
    return moved_rows, reach, plane


def source_rows(rows, centre):
    at = lax.broadcasted_iota(jnp.int32, rows.shape, 0)
    base, reach, plane = centred(rows, centre)
    base = jnp.where(at == 3, reach, jnp.where(at == 7, plane, base))
    a, b, c = split3(base)
    one = jnp.where(at < 3, 1.0, 0.0)
    stacked = jnp.concatenate([a, a, a, b, b, c, one, jnp.zeros_like(one)], axis=0)
    return stacked.astype(jnp.bfloat16), (KAPPA * 0.5) * rows[3:4]


def target_columns(rows, centre):
    at = lax.broadcasted_iota(jnp.int32, rows.shape, 0)
    base, reach, plane = centred(rows, centre)
    zero = jnp.zeros_like(base)
    swapped = pltpu.roll(base, 4, 0)
    facing = jnp.where(at < 3, swapped, 0.0) * (1.0 / math.pi)
    seen = jnp.where((at >= 4) & (at < 7), swapped, jnp.where(at == 7, 1.0, 0.0))
    spread = jnp.where(at < 3, -2.0 * base, jnp.where(at == 3, 1.0, 0.0))
    columns = []
    for factor, constant in ((facing, plane * (1.0 / math.pi)), (seen, None), (spread, reach)):
        a, b, c = split3(factor)
        last = zero
        if constant is not None:
            d, e, f = split3(constant)
            last = jnp.where(at == 0, d, jnp.where(at == 1, e, jnp.where(at == 2, f, 0.0)))
        stacked = jnp.concatenate([a, b, c, a, b, a, last, zero], axis=0)
        columns.append(jnp.transpose(stacked).astype(jnp.bfloat16))
    return columns, (KAPPA * 0.5) * rows[3:4]


def prepare_targets(geo_ref, centre_ref, column_ref, offset_ref):
    for t in range(8):
        rows = block_of(geo_ref, my_block() + t)
        at = lax.broadcasted_iota(jnp.int32, rows.shape, 0)
        centre = jnp.where(at < 3, jnp.broadcast_to(rows[:, 0:1], rows.shape), 0.0)
        centre_ref[t] = centre
        columns, offset = target_columns(rows, centre)
        for r in range(0, BLK, CHUNK):
            column_ref[t, 3 * r : 3 * (r + CHUNK)] = jnp.concatenate(
                [c[r : r + CHUNK] for c in columns], axis=0
            )
        offset_ref[t] = jnp.transpose(jnp.broadcast_to(offset, (HALF, BLK)))


def build_tile(t, b, geo_ref, centre_ref, column_ref, offset_ref, tile_ref, slot):
    source, source_offset = source_rows(block_of(geo_ref, b), centre_ref[t])
    for r in range(0, BLK, CHUNK):
        terms = jnp.dot(
            column_ref[t, 3 * r : 3 * (r + CHUNK), :], source, preferred_element_type=jnp.float32
        )
        facing, seen, spread = terms[:CHUNK], terms[CHUNK : 2 * CHUNK], terms[2 * CHUNK :]
        offset = offset_ref[t, r : r + CHUNK, :]
        offset = jnp.concatenate([offset, offset], axis=1)
        over = jnp.maximum(facing, 0.0) * jnp.maximum(seen, 0.0)
        under = spread * ((spread - offset) - source_offset)
        tile_ref[slot, r : r + CHUNK, :] = (over / under).astype(jnp.bfloat16)


def add_product(t, flux, tile, sum_ref):
    term = lax.dot_general(
        flux, tile, (((1,), (1,)), ((), ())), preferred_element_type=jnp.float32
    )
    sum_ref[t, 0] += term[:, :HALF]
    sum_ref[t, 1] += term[:, HALF:]


def decode(code):
    t = lax.shift_right_logical(code, 10)
    return t, jnp.minimum(t, 7), lax.bitwise_and(code, 1023)


def first_kernel(
    geo_ref, flux_ref, emission_all, material_all, table_all,
    leaving_ref, tiles_ref, list_ref, count_ref, kept_ref,
    emission_ref, material_ref, table_ref, load_sem, code_ref, entry_ref, slot_ref, slot_sem, centre_ref, column_ref, offset_ref, sum_ref, *rest,
):
    bufs, sem = rest[:STEP], rest[STEP]
    loads = [
        pltpu.make_async_copy(emission_all, emission_ref, load_sem.at[0]),
        pltpu.make_async_copy(material_all, material_ref, load_sem.at[1]),
        pltpu.make_async_copy(table_all, table_ref, load_sem.at[2]),
    ]
    for load in loads:
        load.start()
    first = my_block()
    peers = geo_ref.shape[0] // 8
    peer = lax.broadcasted_iota(jnp.int32, (1, peers), 1)
    at_me = lax.broadcasted_iota(jnp.int32, (8, HALF), 1) == lax.div(first, 8)
    pick = jnp.where(at_me, 1.0, 0.0).astype(jnp.bfloat16)
    entry_ref[...] = jnp.full_like(entry_ref, -1)
    for c in range(2):
        for p in range(peers):
            code_ref[p : p + 1, :] = geo_ref[p * 8, c, 7:8, :]
        served = lax.dot_general(
            pick,
            code_ref[...].astype(jnp.bfloat16),
            (((1,), (1,)), ((), ())),
            preferred_element_type=jnp.float32,
        )[0:1].astype(jnp.int32)
        owned = geo_ref[first, c, 7:8, :].astype(jnp.int32)
        for row, code, own in ((c, owned, True), (2 + c, served, False)):
            high, low = lax.shift_right_arithmetic(code, 3), lax.bitwise_and(code, 7)
            target, source = (high, low) if own else (low, high)
            entry_ref[row : row + 1, :] = jnp.where(
                code >= 0, target * 1024 + peer * 8 + source, -1
            )
    slot_copy = pltpu.make_async_copy(entry_ref, slot_ref, slot_sem)
    slot_copy.start()
    prepare_targets(geo_ref, centre_ref, column_ref, offset_ref)
    sum_ref[...] = jnp.zeros_like(sum_ref)
    slot_copy.wait()
    bufs[-1][1] = jnp.zeros_like(bufs[-1][1])

    def compact(e, n):
        for k in range(8):
            code = slot_ref[lax.div(e, HALF // 8), lax.rem(e, HALF // 8) * 8 + k]
            list_ref[n] = code
            n = n + jnp.where(code >= 0, 1, 0)
        return n

    n = lax.fori_loop(0, 4 * HALF // 8, compact, 0)
    for k in range(STEP2):
        list_ref[n + k] = SKIP
    count_ref[0] = n

    @pl.when(n > KEPT)
    def _():
        keep = pltpu.make_async_copy(geo_ref, kept_ref, slot_sem)
        keep.start()
        keep.wait()

    rounds = lax.div(n, STEP)
    rest = n - rounds * STEP

    def out_copy(i, k):
        side = lax.rem(i, 2)
        to = jnp.minimum(i * STEP + k, KEPT)
        return pltpu.make_async_copy(bufs[k].at[side], tiles_ref.at[to], sem.at[side, k])

    def add_tile(code, k, side):
        t, held, b = decode(code)
        add_product(t, block_of(flux_ref, b), bufs[k][side], sum_ref)

    def step(i, carry):
        @pl.when(i >= 2)
        def _():
            for k in range(STEP):
                out_copy(i - 2, k).wait()

        side = lax.rem(i, 2)
        before = jnp.where(i > 0, list_ref[jnp.maximum(i * STEP - 1, 0)], SKIP)
        for k in range(STEP):
            code = list_ref[i * STEP + k]
            t, held, b = decode(code)
            build_tile(held, b, geo_ref, centre_ref, column_ref, offset_ref, bufs[k], side)
            if k == 0:
                add_tile(before, STEP - 1, 1 - side)
            else:
                add_tile(before, k - 1, side)
            before = code
        for k in range(STEP):
            out_copy(i, k).start()
        return carry

    lax.fori_loop(0, rounds, step, 0)
    last = jnp.where(rounds > 0, list_ref[jnp.maximum(rounds * STEP - 1, 0)], SKIP)
    add_tile(last, STEP - 1, lax.rem(rounds + 1, 2))

    @pl.when(rounds >= 2)
    def _():
        for k in range(STEP):
            out_copy(rounds - 2, k).wait()

    side = lax.rem(rounds, 2)
    for low in range(0, STEP, TAIL):

        @pl.when(rest > low)
        def _():
            codes = [list_ref[rounds * STEP + k] for k in range(low, low + TAIL)]
            for k in range(low, low + TAIL):
                t, held, b = decode(codes[k - low])
                build_tile(held, b, geo_ref, centre_ref, column_ref, offset_ref, bufs[k], side)
                if k > low:
                    add_tile(codes[k - low - 1], k - 1, side)
                out_copy(rounds, k).start()
            add_tile(codes[-1], low + TAIL - 1, side)

    @pl.when(rounds >= 1)
    def _():
        for k in range(STEP):
            out_copy(rounds - 1, k).wait()

    for low in range(0, STEP, TAIL):

        @pl.when(rest > low)
        def _():
            for k in range(low, low + TAIL):
                out_copy(rounds, k).wait()

    for load in loads:
        load.wait()
    for u in range(16):
        lanes = slice(u * HALF, (u + 1) * HALF)
        reflect = reflect_of(table_ref, material_ref, lanes)
        radiosity = emission_ref[:, lanes] + reflect * sum_ref[u // 2, u % 2]
        area = geo_ref[first + u // 2, u % 2, 3:4, :]
        leaving_ref[u] = (area * radiosity).astype(jnp.bfloat16)


def second_kernel(
    list_ref, count_ref, geo_all, flux_ref, emission_ref, material_ref, table_ref, tiles_ref,
    out_ref,
    geo_ref, load_sem, centre_ref, column_ref, offset_ref, sum_ref, spare_ref, buf_ref, sem,
):
    n = count_ref[0]
    rounds = pl.cdiv(jnp.minimum(n, KEPT), STEP2)

    def in_copy(i):
        side = lax.rem(i, DEPTH)
        return pltpu.make_async_copy(
            tiles_ref.at[pl.ds(i * STEP2, STEP2)], buf_ref.at[side], sem.at[side]
        )

    for i in range(DEPTH - 1):

        @pl.when(i < rounds)
        def _():
            in_copy(i).start()

    sum_ref[...] = jnp.zeros_like(sum_ref)
    for u in range(16):
        lanes = slice(u * HALF, (u + 1) * HALF)
        out_ref[:, lanes] = reflect_of(table_ref, material_ref, lanes)

    def step(i, carry):
        @pl.when(i + DEPTH - 1 < rounds)
        def _():
            in_copy(i + DEPTH - 1).start()

        in_copy(i).wait()
        side = lax.rem(i, DEPTH)
        for k in range(STEP2):
            t, held, b = decode(list_ref[i * STEP2 + k])
            add_product(t, block_of(flux_ref, b), buf_ref[side, k], sum_ref)
        return carry

    lax.fori_loop(0, rounds, step, 0)

    @pl.when(n > KEPT)
    def _():
        again_load = pltpu.make_async_copy(geo_all, geo_ref, load_sem)
        again_load.start()
        again_load.wait()
        prepare_targets(geo_ref, centre_ref, column_ref, offset_ref)

        def again(e, carry):
            t, held, b = decode(list_ref[e])
            build_tile(held, b, geo_ref, centre_ref, column_ref, offset_ref, spare_ref, 0)
            add_product(t, block_of(flux_ref, b), spare_ref[0], sum_ref)
            return carry

        lax.fori_loop(KEPT, n, again, 0)

    for u in range(16):
        lanes = slice(u * HALF, (u + 1) * HALF)
        out_ref[:, lanes] = emission_ref[:, lanes] + out_ref[:, lanes] * sum_ref[u // 2, u % 2]


def per_device(
    positions, normals, emission, material, area_level, reflect_table, area_table, pair_slots
):
    patches = positions.shape[1]
    units = patches // HALF
    peers = pair_slots.shape[1]
    blocks = peers * 8
    vmem = pl.BlockSpec(memory_space=pltpu.VMEM)
    smem = pl.BlockSpec(memory_space=pltpu.SMEM)
    anywhere = pl.BlockSpec(memory_space=pl.ANY)
    resident = pl.BlockSpec(memory_space=pltpu.HBM)
    material, level = material.reshape(1, patches), area_level.reshape(1, patches)
    slots = jnp.transpose(pair_slots[0], (1, 2, 0))
    pin = lambda x: pltpu.with_memory_space_constraint(x, pltpu.HBM)
    geo_units = jax.ShapeDtypeStruct((units, 8, HALF), jnp.float32)
    flux_units = jax.ShapeDtypeStruct((units, BANDS, HALF), jnp.bfloat16)
    geo, flux = gather_all(
        [geo_units, flux_units],
        FIRST_PARTS,
        0,
        [resident] * 6,
        [pin(x) for x in (positions, normals, emission, level, area_table.reshape(1, -1), slots)],
        own_first,
    )
    geo = geo.reshape(blocks, 2, 8, HALF)

    scratch = [
        pltpu.VMEM((8, 8, BLK), jnp.float32),
        pltpu.VMEM((8, 3 * BLK, 64), jnp.bfloat16),
        pltpu.VMEM((8, BLK, HALF), jnp.float32),
        pltpu.VMEM((9, 2, BANDS, HALF), jnp.float32),
    ]
    leaving, tiles, listed, counted, kept = pl.pallas_call(
        first_kernel,
        out_shape=[
            jax.ShapeDtypeStruct((units, BANDS, HALF), jnp.bfloat16),
            jax.ShapeDtypeStruct((KEPT + STEP2, BLK, BLK), jnp.bfloat16),
            jax.ShapeDtypeStruct((4 * peers + STEP2,), jnp.int32),
            jax.ShapeDtypeStruct((1,), jnp.int32),
            jax.ShapeDtypeStruct(geo.shape, jnp.float32),
        ],
        in_specs=[vmem] * 2 + [resident] * 3,
        out_specs=[vmem, anywhere, smem, smem, anywhere],
        scratch_shapes=[
            pltpu.VMEM(emission.shape, jnp.float32),
            pltpu.VMEM(material.shape, jnp.int32),
            pltpu.VMEM(reflect_table.shape, jnp.float32),
            pltpu.SemaphoreType.DMA((3,)),
            pltpu.VMEM((peers, HALF), jnp.float32),
            pltpu.VMEM((8, peers), jnp.int32),
            pltpu.SMEM((8, peers), jnp.int32),
            pltpu.SemaphoreType.DMA(()),
        ]
        + scratch
        + [pltpu.VMEM((2, BLK, BLK), jnp.bfloat16)] * STEP
        + [pltpu.SemaphoreType.DMA((2, STEP))],
        compiler_params=pltpu.CompilerParams(vmem_limit_bytes=20 << 20),
        name="first_sweep",
    )(geo, flux.reshape(blocks, 2, BANDS, HALF), pin(emission), pin(material), pin(reflect_table))
    (flux,) = gather_all(
        [flux_units], LATER_PARTS, 1, [anywhere], [leaving], short=True
    )
    return pl.pallas_call(
        second_kernel,
        out_shape=jax.ShapeDtypeStruct((BANDS, patches), jnp.float32),
        in_specs=[smem, smem, anywhere] + [vmem] * 4 + [anywhere],
        out_specs=vmem,
        scratch_shapes=[
            pltpu.VMEM((blocks, 2, 8, HALF), jnp.float32),
            pltpu.SemaphoreType.DMA(()),
        ]
        + scratch
        + [
            pltpu.VMEM((1, BLK, BLK), jnp.bfloat16),
            pltpu.VMEM((DEPTH, STEP2, BLK, BLK), jnp.bfloat16),
            pltpu.SemaphoreType.DMA((DEPTH,)),
        ],
        compiler_params=pltpu.CompilerParams(vmem_limit_bytes=34 << 20),
        name="second_sweep",
    )(
        listed, counted, kept, flux.reshape(blocks, 2, BANDS, HALF), emission, material,
        reflect_table, tiles,
    )


def solution(mesh):
    placed = (
        P(None, AXES),
        P(None, AXES),
        P(None, AXES),
        P(AXES),
        P(AXES),
        P(),
        P(),
        P(AXES, None, None, None),
    )
    return jax.shard_map(
        per_device, mesh=mesh, in_specs=placed, out_specs=P(None, AXES), check_vma=False
    )
```
